128 devices in a mesh: cell: 64 (over y, z, x), qgrp: 2 (over core).
Axes of the slice: x: 4, y: 4, z: 4, core: 2. Of those that a mesh axis runs over, the one named last changes fastest.
Arguments:
- supernode_embeddings: bfloat16 [32768, 768], P('cell'), may hold values from -6 to 6
- filled_supernode_tally: int32 [64], P('cell'), may hold values from 1 to 512, 24576 in all
- hidden_probe_states: bfloat16 [1024, 768], replicated, may hold values from -6 to 6
- softness_per_channel: float32 [2, 12], replicated, may hold values from 1 to 12, as said below
- gather_probe_projector: bfloat16 [768, 768], P(None, 'qgrp'), may hold values from -0.4375 to 0.4375
- gather_lookup_projector: bfloat16 [768, 768], P(None, 'qgrp'), may hold values from -0.4375 to 0.4375
- gather_content_projector: bfloat16 [768, 768], P(None, 'qgrp'), may hold values from -0.21875 to 0.21875
- gather_final_projector: bfloat16 [768, 768], P('qgrp'), may hold values from -0.21875 to 0.21875
- unpack_probe_projector: bfloat16 [768, 768], P(None, 'qgrp'), may hold values from -0.21875 to 0.21875
- unpack_lookup_projector: bfloat16 [768, 768], P(None, 'qgrp'), may hold values from -0.21875 to 0.21875
- unpack_content_projector: bfloat16 [768, 768], P(None, 'qgrp'), may hold values from -0.21875 to 0.21875
- unpack_final_projector: bfloat16 [768, 768], P('qgrp'), may hold values from -0.21875 to 0.21875
- hidden_state_gain: float32 [768], replicated, may hold values from 0.1 to 1.9
Outputs:
- latent_out: float32 [1024, 768], replicated
- tokens_out: float32 [32768, 768], P(('cell', 'qgrp'))
The draws below stay inside these ranges and needn't reach their ends.
Inputs may be any that keep to these rules, and one draw needn't show every extreme that they name: Slots 0 to filled_supernode_tally[c] - 1 of cell block c hold its valid supernodes; its other slots are padding. `softness_per_channel`: A positive temperature for each head.
All inputs are finite; a program needn't handle non-finite values.
Results may differ from the reference program's by a relative error of at most 0.009.
The reference program's roundings to bfloat16 on the way count: a program that leaves them out, or rounds other values in their place, can miss the bound.
Values may be sent and summed in bfloat16 or wider, within the bound.
A program may use at most 448 MiB of HBM per device.

```python
import math
import jax
import jax.numpy as jnp
import numpy as np
from jax import lax

D = 768
HEADS = 12
L = 1024
CAP = 512
NTOK = 32768
N_CELL = 64


def draw_softness_per_channel(key, part):
    base = jax.random.uniform(key, (2, HEADS), jnp.float32)
    return jnp.exp(base * math.log(3.0))


def level_of(own_key, extent, pieces, least, top_value):
    def one(position, shards_of):
        steps = jax.random.uniform(jax.random.fold_in(jax.random.fold_in(own_key, 6), position), (shards_of,), jnp.float32, least / len(pieces), top_value / len(pieces))
        return jnp.repeat(jnp.exp(steps), extent[position] // shards_of).reshape((-1,) + (1,) * (len(extent) - position - 1))

    loudness = one(*pieces[0])
    for cut in pieces[1:]:
        loudness = loudness * one(*cut)
    return loudness


def profile(count, total, bound, slope):
    portions = [(1 << 20) // math.isqrt(rank ** slope) + 1 for rank in range(2, count + 1)]
    surplus, counts = total - bound - (count - 1), [1] * (count - 1)
    while surplus > 0:
        candidates = [i for i in range(count - 1) if counts[i] < bound]
        pool, budget = sum([portions[i] for i in candidates]), surplus
        for i in candidates:
            addition = min(bound - counts[i], max(1, budget * portions[i] // pool), surplus)
            counts[i] = counts[i] + addition
            surplus = surplus - addition
    return np.array([bound] + counts)


def uneven(stream_key, amount, total, reach, slope):
    if amount == 2:
        one = jax.random.randint(stream_key, (), max(1, total - reach), min(reach, total - 1) + 1)
        return jnp.stack([one, total - one])
    tallies = jnp.asarray(profile(amount, total, reach, slope), jnp.int32)
    pairs = (amount - 1) // 2
    source_of, receiver = tallies[1:1 + 2 * pairs:2], tallies[2:2 + 2 * pairs:2]
    slack = jnp.minimum(source_of - 1, reach - receiver)
    passed = jax.random.randint(jax.random.fold_in(stream_key, 1), (pairs,), 0, 1 << 20) % (slack + 1)
    tallies = tallies.at[1:1 + 2 * pairs:2].set(source_of - passed).at[2:2 + 2 * pairs:2].set(receiver + passed)
    return tallies[jax.random.permutation(jax.random.fold_in(stream_key, 2), amount)]


def scatter_about(own_key, extent, spread, limit, split=(), kind=jnp.bfloat16):
    loudness = level_of(own_key, extent, split, -0.22, 0.18) if split else 1.0
    entries = jax.random.normal(own_key, extent, jnp.float32) * spread * loudness
    return jnp.minimum(jnp.maximum(entries, -limit), limit).astype(kind)


def setup_inputs(seed: int = 0) -> dict:
    seeds = jax.random.split(jax.random.key(seed), 14)
    supernode_embeddings = scatter_about(seeds[0], (NTOK, D), 1.0, 6.0, ((0, 64),))
    filled_supernode_tally = uneven(seeds[1], N_CELL, 3 * N_CELL * CAP // 4, CAP, 1).astype(jnp.int32)
    hidden_probe_states = scatter_about(seeds[2], (L, D), 1.0, 6.0)
    softness_per_channel = draw_softness_per_channel(jax.random.fold_in(seeds[13], 71), 0)
    gather_probe_projector = scatter_about(seeds[4], (D, D), (D // 4) ** -0.5, 0.4375, ((1, 2),))
    gather_lookup_projector = scatter_about(seeds[5], (D, D), (D // 4) ** -0.5, 0.4375, ((1, 2),))
    gather_content_projector = scatter_about(seeds[6], (D, D), D ** -0.5, 0.21875, ((1, 2),))
    gather_final_projector = scatter_about(seeds[7], (D, D), D ** -0.5, 0.21875, ((0, 2),))
    unpack_probe_projector = scatter_about(seeds[8], (D, D), D ** -0.5, 0.21875, ((1, 2),))
    unpack_lookup_projector = scatter_about(seeds[9], (D, D), D ** -0.5, 0.21875, ((1, 2),))
    unpack_content_projector = scatter_about(seeds[10], (D, D), D ** -0.5, 0.21875, ((1, 2),))
    unpack_final_projector = scatter_about(seeds[11], (D, D), D ** -0.5, 0.21875, ((0, 2),))
    hidden_state_gain = jnp.clip(1.0 + 0.18 * jax.random.normal(seeds[12], (D,), jnp.float32), 0.1, 1.9)
    return dict(supernode_embeddings=supernode_embeddings, filled_supernode_tally=filled_supernode_tally, hidden_probe_states=hidden_probe_states, softness_per_channel=softness_per_channel, gather_probe_projector=gather_probe_projector, gather_lookup_projector=gather_lookup_projector, gather_content_projector=gather_content_projector, gather_final_projector=gather_final_projector, unpack_probe_projector=unpack_probe_projector, unpack_lookup_projector=unpack_lookup_projector, unpack_content_projector=unpack_content_projector, unpack_final_projector=unpack_final_projector, hidden_state_gain=hidden_state_gain)


MASKED_SCORE = -1e+30
NORM_EPSILON = 1e-06

def rounded(values):
    return lax.optimization_barrier(values.astype(jnp.bfloat16)).astype(jnp.float32)

def rms_norm(values, gain):
    mean_square = lax.optimization_barrier(jnp.mean(values * values, axis=-1, keepdims=True))
    return values * lax.rsqrt(mean_square + NORM_EPSILON) * gain

def reference(supernode_embeddings, filled_supernode_tally, hidden_probe_states, softness_per_channel, gather_probe_projector, gather_lookup_projector, gather_content_projector, gather_final_projector, unpack_probe_projector, unpack_lookup_projector, unpack_content_projector, unpack_final_projector, hidden_state_gain):
    per_channel_dimension = D // HEADS
    gather_multiplier = softness_per_channel[0] * per_channel_dimension ** (-0.5)
    unpack_multiplier = softness_per_channel[1] * per_channel_dimension ** (-0.5)
    queries = rounded(jnp.dot(hidden_probe_states, gather_probe_projector, preferred_element_type=jnp.float32)).reshape(L, HEADS, per_channel_dimension)
    cell_tokens = supernode_embeddings.reshape(N_CELL, CAP, D)

    def visit(running, item):
        run_max, run_sum, run_acc = running
        block_tokens, live_count = item
        key_rows = rounded(jnp.dot(block_tokens, gather_lookup_projector, preferred_element_type=jnp.float32)).reshape(CAP, HEADS, per_channel_dimension)
        value_rows = rounded(jnp.dot(block_tokens, gather_content_projector, preferred_element_type=jnp.float32)).reshape(CAP, HEADS, per_channel_dimension)
        is_valid = lax.iota(jnp.int32, CAP) < live_count
        scores = jnp.einsum('lhd,khd->lhk', queries, key_rows) * gather_multiplier[None, :, None]
        scores = jnp.where(is_valid[None, None, :], scores, jnp.float32(MASKED_SCORE))
        block_max = lax.optimization_barrier(jnp.max(scores, axis=-1))
        weights = jnp.exp(scores - block_max[:, :, None]) * is_valid[None, None, :].astype(jnp.float32)
        block_sum = lax.optimization_barrier(jnp.sum(weights, axis=-1))
        block_acc = jnp.einsum('lhk,khd->lhd', rounded(weights), value_rows)
        new_max = jnp.maximum(run_max, block_max)
        old_factor = jnp.exp(run_max - new_max)
        block_factor = jnp.exp(block_max - new_max)
        new_sum = run_sum * old_factor + block_sum * block_factor
        new_acc = run_acc * old_factor[:, :, None] + block_acc * block_factor[:, :, None]
        return ((new_max, new_sum, new_acc), None)
    initial = (jnp.full((L, HEADS), MASKED_SCORE, jnp.float32), jnp.zeros((L, HEADS), jnp.float32), jnp.zeros((L, HEADS, per_channel_dimension), jnp.float32))
    (run_max, run_sum, run_acc), unused = lax.scan(visit, initial, (cell_tokens, filled_supernode_tally.astype(jnp.int32)))
    attended = (run_acc / run_sum[:, :, None]).astype(jnp.bfloat16).reshape(L, D)
    latent_pre = hidden_probe_states.astype(jnp.float32) + jnp.dot(attended, gather_final_projector, preferred_element_type=jnp.float32)
    latent_out = rms_norm(latent_pre, hidden_state_gain)
    latent_half = latent_out.astype(jnp.bfloat16)
    dec_keys = rounded(jnp.dot(latent_half, unpack_lookup_projector, preferred_element_type=jnp.float32)).reshape(L, HEADS, per_channel_dimension)
    dec_values = rounded(jnp.dot(latent_half, unpack_content_projector, preferred_element_type=jnp.float32)).reshape(L, HEADS, per_channel_dimension)

    def decode_cell(item):
        block_tokens, live_count = item
        dec_queries = rounded(jnp.dot(block_tokens, unpack_probe_projector, preferred_element_type=jnp.float32)).reshape(CAP, HEADS, per_channel_dimension)
        scores = jnp.einsum('khd,lhd->khl', dec_queries, dec_keys) * unpack_multiplier[None, :, None]
        weights = jnp.exp(scores - lax.optimization_barrier(jnp.max(scores, axis=-1, keepdims=True)))
        denominator = lax.optimization_barrier(jnp.sum(weights, axis=-1))
        mixed_heads = jnp.einsum('khl,lhd->khd', rounded(weights), dec_values) / denominator[:, :, None]
        dec_att = mixed_heads.astype(jnp.bfloat16).reshape(CAP, D)
        update = jnp.dot(dec_att, unpack_final_projector, preferred_element_type=jnp.float32)
        is_valid = lax.iota(jnp.int32, CAP) < live_count
        return jnp.where(is_valid[:, None], block_tokens.astype(jnp.float32) + update, jnp.float32(0.0))
    tokens_out = lax.map(decode_cell, (cell_tokens, filled_supernode_tally.astype(jnp.int32))).reshape(N_CELL * CAP, D)
    return (latent_out, tokens_out)
```

```python
import functools
import math

import jax
import jax.numpy as jnp
from jax import lax
from jax.experimental import pallas as pl
from jax.experimental.pallas import tpu as pltpu
from jax.sharding import PartitionSpec as P

D = 768
HEADS = 12
HD = 64
MASKED = -1e30
EPS = 1e-06
LOG2E = math.log2(math.e)
MESH = pl.DeviceIdType.MESH
F32 = jnp.float32
BF16 = jnp.bfloat16
VMEM = pl.BlockSpec(memory_space=pltpu.VMEM)
SMEM = pl.BlockSpec(memory_space=pltpu.SMEM)
ANY = pl.BlockSpec(memory_space=pl.ANY)
LIMIT = 60 * 1024 * 1024


def dot(a, b):
    return jnp.dot(a, b, preferred_element_type=F32)


def dot_nt(a, b):
    return lax.dot_general(a, b, (((1,), (1,)), ((), ())), preferred_element_type=F32)


def lanes(shape):
    return lax.broadcasted_iota(jnp.int32, shape, len(shape) - 1)


def three(x):
    high = x.astype(BF16).astype(F32)
    rest = x - high
    middle = rest.astype(BF16).astype(F32)
    return high, middle, rest - middle


def encoder(emb, tally, hidden, soft, wq, wk, wv, out, q_scr, k_scr, v_scr, m_scr, d_scr):
    rows, group = hidden.shape[0], wq.shape[1]
    slots = emb.shape[0]
    pairs = group // 128
    first_head = lax.axis_index("qgrp") * (2 * pairs)
    q_scr[...] = dot(hidden[...], wq[...]).astype(BF16)
    keys = dot(emb[...], wk[...])
    low = lanes((1, group)) % 128 < HD
    k_scr[0] = jnp.where(low, keys, 0.0).astype(BF16)
    k_scr[1] = jnp.where(low, 0.0, keys).astype(BF16)
    values = dot(emb[...], wv[...]).astype(BF16)
    for pair in range(pairs):
        v_scr[pair, :, :128] = values[:, pair * 128 : (pair + 1) * 128]
        v_scr[pair, :, 128:] = jnp.ones((slots, 128), BF16)
    bias = jnp.where(lanes((1, slots)) < tally[0], 0.0, MASKED)
    m_scr[...] = jnp.zeros_like(m_scr)
    d_scr[...] = jnp.zeros_like(d_scr)
    tile = 256

    @pl.loop(0, pairs)
    def _(pair):
        at = pl.ds(pl.multiple_of(pair * 128, 128), 128)
        for start in range(0, rows, tile):
            span = slice(start, start + tile)
            halves = []
            for part in range(2):
                head = 2 * pair + part
                scale = soft[0, first_head + head] * HD**-0.5
                scores = dot_nt(q_scr[span, at], k_scr[part, :, at]) + bias
                top = jnp.max(scores, axis=-1, keepdims=True)
                weights = jnp.exp2((scores - top) * (scale * LOG2E)).astype(BF16)
                halves.append(dot(weights, v_scr[pair]))
                here = lanes((tile, 128)) == head
                m_scr[span, :] = jnp.where(here, top * scale, m_scr[span, :])
                d_scr[span, :] = jnp.where(here, halves[-1][:, 128:], d_scr[span, :])
            mixed = jnp.where(lanes((tile, 128)) < HD, halves[0][:, :128], halves[1][:, :128])
            out[span, at] = mixed.astype(BF16)

    parts = three(m_scr[...]) + three(d_scr[...])
    packed = parts[0]
    for place in range(1, 6):
        packed = packed + pltpu.roll(parts[place], 16 * place, 1)
    out[:, group:] = packed.astype(BF16)


def exchange(
    n,
    msg, hidden, wo, gain, dq, dk, dv, do,
    latents, tq, tk, tv, to,
    inbox, rows_scr, mine, theirs,
    send_sem, recv_sem, pair_send, pair_recv, local_sem, fwd_send, fwd_recv,
):
    cell, core = lax.axis_index("cell"), lax.axis_index("qgrp")
    partner = (cell, 1 - core)
    rows = inbox.shape[1]
    group = wo.shape[0]

    barrier = pltpu.get_barrier_semaphore()

    @pl.loop(1, n)
    def _(step):
        to_cell = lax.rem(cell + step, n)
        pl.semaphore_signal(barrier, inc=1, device_id=(to_cell, core), device_id_type=MESH)

    pl.semaphore_signal(barrier, inc=1, device_id=partner, device_id_type=MESH)
    own = pltpu.make_async_copy(hidden.at[pl.ds(pl.multiple_of(cell * rows, rows), rows)], rows_scr, local_sem.at[0])
    own.start()
    keep = pltpu.make_async_copy(msg.at[cell], inbox.at[cell], local_sem.at[1])
    keep.start()
    pl.semaphore_wait(barrier, n)

    def deal(step):
        to_cell = lax.rem(cell + step, n)
        return pltpu.make_async_remote_copy(
            src_ref=msg.at[to_cell], dst_ref=inbox.at[cell],
            send_sem=send_sem.at[step], recv_sem=recv_sem.at[cell],
            device_id=(to_cell, core), device_id_type=MESH,
        )

    @pl.loop(1, n)
    def _(step):
        deal(step).start()

    weights = [
        pltpu.make_async_remote_copy(
            src_ref=source, dst_ref=target, send_sem=pair_send.at[i], recv_sem=pair_recv.at[i],
            device_id=partner, device_id_type=MESH,
        )
        for i, (source, target) in enumerate(((dq, tq), (dk, tk), (dv, tv), (do, to)))
    ]
    for copy in weights:
        copy.start()
    keep.wait()

    @pl.loop(1, n)
    def _(step):
        source = lax.rem(cell + step, n)
        pltpu.make_async_remote_copy(
            src_ref=msg.at[source], dst_ref=inbox.at[source],
            send_sem=send_sem.at[step], recv_sem=recv_sem.at[source],
            device_id=(source, core), device_id_type=MESH,
        ).wait_recv()

    stats = inbox[:, :, group:].astype(F32).reshape(n * rows, 128)
    top = stats + pltpu.roll(stats, 112, 1) + pltpu.roll(stats, 96, 1)
    total = pltpu.roll(stats, 80, 1) + pltpu.roll(stats, 64, 1) + pltpu.roll(stats, 48, 1)
    used = lanes((n * rows, 128)) < group // HD
    top = jnp.where(used, top, 0.0).reshape(n, rows, 128)
    total = jnp.where(used, total, 0.0).reshape(n, rows, 128)
    factor = jnp.exp(top - jnp.max(top, axis=0, keepdims=True)).astype(BF16)
    total = jnp.sum(factor.astype(F32) * total, axis=0)
    spread = (
        lax.broadcasted_iota(jnp.int32, (128, group), 0) == lanes((128, group)) // HD
    ).astype(BF16)
    wide = dot(factor.reshape(n * rows, 128), spread).reshape(n, rows, group)
    summed = jnp.sum(wide * inbox[:, :, :group].astype(F32), axis=0)
    divisor = sum(dot(part.astype(BF16), spread) for part in three(total))
    attended = (summed / divisor).astype(BF16)
    mine[...] = dot(attended, wo[...])
    swap = pltpu.make_async_remote_copy(
        src_ref=mine, dst_ref=theirs, send_sem=pair_send.at[4], recv_sem=pair_recv.at[4],
        device_id=partner, device_id_type=MESH,
    )
    swap.start()
    own.wait()
    swap.wait()
    before = rows_scr[...].astype(F32) + (mine[...] + theirs[...])
    square = jnp.mean(before * before, axis=-1, keepdims=True)
    latents[cell] = (before * lax.rsqrt(square + EPS) * gain[...]).astype(BF16)

    half = pl.ds(pl.multiple_of(core * group, 128), group)
    other = pl.ds(pl.multiple_of((1 - core) * group, 128), group)

    def share(step):
        to_cell = lax.rem(cell + step, n)
        return pltpu.make_async_remote_copy(
            src_ref=latents.at[cell, :, half], dst_ref=latents.at[cell, :, half],
            send_sem=send_sem.at[n + step], recv_sem=recv_sem.at[n + cell],
            device_id=(to_cell, core), device_id_type=MESH,
        )

    def landed(source):
        return pltpu.make_async_remote_copy(
            src_ref=latents.at[source, :, half], dst_ref=latents.at[source, :, half],
            send_sem=send_sem.at[n], recv_sem=recv_sem.at[n + source],
            device_id=(source, core), device_id_type=MESH,
        )

    def forward(source, part):
        return pltpu.make_async_remote_copy(
            src_ref=latents.at[source, :, part], dst_ref=latents.at[source, :, part],
            send_sem=fwd_send.at[source], recv_sem=fwd_recv.at[source],
            device_id=partner, device_id_type=MESH,
        )

    @pl.loop(1, n)
    def _(step):
        share(step).start()

    @pl.loop(1, n)
    def _(step):
        source = lax.rem(cell + n - step, n)
        landed(source).wait_recv()
        forward(source, half).start()

    @pl.loop(1, n)
    def _(step):
        source = lax.rem(cell + n - step, n)
        forward(source, other).wait_recv()

    @pl.loop(1, n)
    def _(step):
        source = lax.rem(cell + n - step, n)
        forward(source, half).wait_send()
        deal(step).wait_send()
        share(step).wait_send()

    for copy in weights:
        copy.wait()


def decoder(lat, emb, tally, soft, q0, q1, k0, k1, v0, v1, o0, o1, latent_out, tokens, k_scr, v_scr, q_scr, a_scr):
    core = lax.axis_index("qgrp")
    rows, group = lat.shape[0], q0.shape[1]
    slots = tokens.shape[0]
    pairs = group // 128
    own = pl.ds(pl.multiple_of(core * slots, slots), slots)
    latent_out[...] = lat[...].astype(F32)
    low = lanes((1, group)) % 128 < HD
    for side, (wq, wk, wv) in enumerate(((q0, k0, v0), (q1, k1, v1))):
        at = slice(side * group, (side + 1) * group)
        q_scr[:, at] = dot(emb[own, :], wq[...]).astype(BF16)
        keys = dot(lat[...], wk[...])
        k_scr[0, :, at] = jnp.where(low, keys, 0.0).astype(BF16)
        k_scr[1, :, at] = jnp.where(low, 0.0, keys).astype(BF16)
        values = dot(lat[...], wv[...]).astype(BF16)
        for pair in range(pairs):
            v_scr[side * pairs + pair, :, :128] = values[:, pair * 128 : (pair + 1) * 128]
            v_scr[side * pairs + pair, :, 128:] = jnp.ones((rows, 128), BF16)

    @pl.loop(0, 2 * pairs)
    def _(pair):
        at = pl.ds(pl.multiple_of(pair * 128, 128), 128)
        side = lax.rem(core + pair // pairs, 2)
        first = side * (2 * pairs) + 2 * lax.rem(pair, pairs)
        halves = []
        for part in range(2):
            scale = soft[1, first + part] * HD**-0.5
            scores = dot_nt(q_scr[:, at], k_scr[part, :, at])
            top = jnp.max(scores, axis=-1, keepdims=True)
            weights = jnp.exp2((scores - top) * (scale * LOG2E)).astype(BF16)
            mixed = dot(weights, v_scr[pair])
            halves.append(mixed[:, :128] / mixed[:, 128:])
        a_scr[:, at] = jnp.where(lanes((slots, 128)) < HD, halves[0], halves[1]).astype(BF16)

    update = dot(a_scr[:, :group], o0[...]) + dot(a_scr[:, group:], o1[...])
    position = core * slots + lax.broadcasted_iota(jnp.int32, (slots, 1), 0)
    tokens[...] = jnp.where(position < tally[0], emb[own, :].astype(F32) + update, 0.0)


def body(n, emb, tally, hidden, soft, gq, gk, gv, go, uq, uk, uv, uo, gain):
    rows, group = hidden.shape[0], gq.shape[1]
    slots = emb.shape[0]
    pairs = group // 128
    msg = pl.pallas_call(
        encoder,
        name="encoder",
        out_shape=jax.ShapeDtypeStruct((rows, group + 128), BF16),
        in_specs=[VMEM, SMEM, VMEM, SMEM, VMEM, VMEM, VMEM],
        out_specs=VMEM,
        scratch_shapes=[
            pltpu.VMEM((rows, group), BF16),
            pltpu.VMEM((2, slots, group), BF16),
            pltpu.VMEM((pairs, slots, 256), BF16),
            pltpu.VMEM((rows, 128), F32),
            pltpu.VMEM((rows, 128), F32),
        ],
        compiler_params=pltpu.CompilerParams(vmem_limit_bytes=LIMIT),
    )(emb, tally, hidden, soft, gq, gk, gv)
    each = rows // n
    dma = pltpu.SemaphoreType.DMA
    like = lambda x: jax.ShapeDtypeStruct(x.shape, x.dtype)
    latents, tq, tk, tv, to = pl.pallas_call(
        functools.partial(exchange, n),
        name="exchange",
        out_shape=(jax.ShapeDtypeStruct((n, each, D), BF16), like(uq), like(uk), like(uv), like(uo)),
        in_specs=[VMEM, ANY, VMEM, VMEM, ANY, ANY, ANY, ANY],
        out_specs=(VMEM, ANY, ANY, ANY, ANY),
        scratch_shapes=[
            pltpu.VMEM((n, each, group + 128), BF16),
            pltpu.VMEM((each, D), BF16),
            pltpu.VMEM((each, D), F32),
            pltpu.VMEM((each, D), F32),
            dma((2 * n,)), dma((2 * n,)), dma((5,)), dma((5,)), dma((2,)), dma((n,)), dma((n,)),
        ],
        compiler_params=pltpu.CompilerParams(collective_id=0, has_side_effects=True, vmem_limit_bytes=LIMIT),
    )(msg.reshape(n, each, group + 128), hidden, go, gain.reshape(1, D), uq, uk, uv, uo)
    half = slots // 2
    return pl.pallas_call(
        decoder,
        name="decoder",
        out_shape=(jax.ShapeDtypeStruct((rows, D), F32), jax.ShapeDtypeStruct((half, D), F32)),
        in_specs=[VMEM, VMEM, SMEM, SMEM] + [VMEM] * 8,
        out_specs=(VMEM, VMEM),
        scratch_shapes=[
            pltpu.VMEM((2, rows, D), BF16),
            pltpu.VMEM((2 * pairs, rows, 256), BF16),
            pltpu.VMEM((half, D), BF16),
            pltpu.VMEM((half, D), BF16),
        ],
        compiler_params=pltpu.CompilerParams(vmem_limit_bytes=LIMIT),
    )(latents.reshape(rows, D), emb, tally, soft, uq, tq, uk, tk, uv, tv, uo, to)


def solution(mesh):
    column, row = P(None, "qgrp"), P("qgrp", None)
    placed = (P("cell", None), P("cell"), P(), P(), column, column, column, row, column, column, column, row, P())
    return jax.shard_map(
        functools.partial(body, mesh.shape["cell"]),
        mesh=mesh,
        in_specs=placed,
        out_specs=(P(), P(("cell", "qgrp"), None)),
        check_vma=False,
    )
```

```python
import functools
import math

import jax
import jax.numpy as jnp
from jax import lax
from jax.experimental import pallas as pl
from jax.experimental.pallas import tpu as pltpu
from jax.sharding import PartitionSpec as P

D = 768
HEADS = 12
HD = 64
RING = 4
COLOURS = 3
REDUCE_AXES = ((0, 1, 2), (1, 2, 0), (2, 0, 1))
GATHER_AXES = ((2, 1, 0), (0, 2, 1), (1, 0, 2))
MASKED = -1e30
EPS = 1e-06
LOG2E = math.log2(math.e)
MESH = pl.DeviceIdType.MESH
F32 = jnp.float32
BF16 = jnp.bfloat16
VMEM = pl.BlockSpec(memory_space=pltpu.VMEM)
SMEM = pl.BlockSpec(memory_space=pltpu.SMEM)
ANY = pl.BlockSpec(memory_space=pl.ANY)
LIMIT = 60 * 1024 * 1024


def dot(a, b):
    return jnp.dot(a, b, preferred_element_type=F32)


def dot_nt(a, b):
    return lax.dot_general(a, b, (((1,), (1,)), ((), ())), preferred_element_type=F32)


def lanes(shape):
    return lax.broadcasted_iota(jnp.int32, shape, len(shape) - 1)


def three(x):
    high = x.astype(BF16).astype(F32)
    rest = x - high
    middle = rest.astype(BF16).astype(F32)
    return high, middle, rest - middle


def packed_stats(top, total):
    place = lanes(top.shape) % HD
    packed = jnp.zeros_like(top)
    for i, part in enumerate(three(top) + three(total)):
        packed = jnp.where(place == i, part, packed)
    return packed.astype(BF16)


def unpacking():
    source = lax.broadcasted_iota(jnp.int32, (128, 256), 0)
    target = lanes((128, 256))
    same = (target % 128) // HD == source // HD
    return (same & ((source % HD) // 3 == target // 128)).astype(BF16)


def merged(box):
    count, rows, _ = box.shape
    stats = dot(box[:, :, 128:].reshape(count * rows, 128), unpacking()).reshape(count, rows, 256)
    top, total = stats[:, :, :128], stats[:, :, 128:]
    best = jnp.max(top, axis=0)
    factor = jnp.exp(top - best)
    return jnp.sum(factor * box[:, :, :128].astype(F32), axis=0), best, jnp.sum(factor * total, axis=0)


def gather(
    emb, tally, hidden, soft, wq, wk, wv, wo, gain, dq, dk, dv, do,
    latents, tq, tk, tv, to,
    q_scr, k_scr, v_scr, out1, box1, out2, box2, out3, box3, mine, theirs,
    red_send, red_recv, gat_send, gat_recv, fwd_send, fwd_recv, pair_send, pair_recv,
):
    cell, core = lax.axis_index("cell"), lax.axis_index("qgrp")
    here = (cell // 16, (cell // 4) % 4, cell % 4)
    partner = (cell, 1 - core)
    rows, group = hidden.shape[0], wq.shape[1]
    slots = emb.shape[0]
    quarter, each = rows // RING, rows // RING**3

    def peer(axis, digit):
        at = [digit if i == axis else here[i] for i in range(3)]
        return ((at[0] * RING + at[1]) * RING + at[2], core)

    def turn(axis, step):
        return lax.rem(here[axis] + step, RING)

    barrier = pltpu.get_barrier_semaphore()
    for axis in range(3):
        for step in range(1, RING):
            pl.semaphore_signal(barrier, inc=1, device_id=peer(axis, turn(axis, step)), device_id_type=MESH)
    pl.semaphore_signal(barrier, inc=1, device_id=partner, device_id_type=MESH)

    queries = dot(hidden[...], wq[...]).astype(BF16)
    keys = dot(emb[...], wk[...])
    low = lanes((1, group)) % 128 < HD
    k_scr[0] = jnp.where(low, keys, 0.0).astype(BF16)
    k_scr[1] = jnp.where(low, 0.0, keys).astype(BF16)
    values = dot(emb[...], wv[...]).astype(BF16)
    for pair in range(COLOURS):
        block = slice(pair * 128, (pair + 1) * 128)
        q_scr[pair] = queries[:, block].reshape(RING, RING, RING, each, 128)
        v_scr[pair, :, :128] = values[:, block]
        v_scr[pair, :, 128:] = jnp.ones((slots, 128), BF16)
    bias = jnp.where(lanes((1, slots)) < tally[0], 0.0, MASKED)
    first_head = core * (2 * COLOURS)

    pl.semaphore_wait(barrier, 10)
    weights = [
        pltpu.make_async_remote_copy(
            src_ref=source, dst_ref=target, send_sem=pair_send.at[i], recv_sem=pair_recv.at[i],
            device_id=partner, device_id_type=MESH,
        )
        for i, (source, target) in enumerate(((dq, tq), (dk, tk), (dv, tv), (do, to)))
    ]
    for copy in weights:
        copy.start()

    def tile(pair, digit):
        axis = REDUCE_AXES[pair][0]
        q = q_scr[(pair,) + tuple(digit if i == axis else slice(None) for i in range(axis + 1))]
        q = q.reshape(quarter, 128)
        first = lanes((quarter, 128)) < HD
        tops, halves = [], []
        for part in range(2):
            scale = soft[0, first_head + 2 * pair + part] * HD**-0.5
            scores = dot_nt(q, k_scr[part, :, pair * 128 : (pair + 1) * 128]) + bias
            top = jnp.max(scores, axis=-1, keepdims=True)
            weight = jnp.exp2((scores - top) * (scale * LOG2E)).astype(BF16)
            halves.append(dot(weight, v_scr[pair]))
            tops.append(top * scale)
        mixed = jnp.where(first, halves[0][:, :128], halves[1][:, :128])
        total = jnp.where(first, halves[0][:, 128:], halves[1][:, 128:])
        return mixed.astype(BF16), packed_stats(jnp.where(first, tops[0], tops[1]), total)

    outs, boxes = (out1, out2, out3), (box1, box2, box3)

    def reduce_copy(stage, pair, digit):
        axis = REDUCE_AXES[pair][stage]
        return pltpu.make_async_remote_copy(
            src_ref=outs[stage].at[pair, digit], dst_ref=boxes[stage].at[pair, here[axis]],
            send_sem=red_send.at[stage, pair, digit], recv_sem=red_recv.at[stage, pair, here[axis]],
            device_id=peer(axis, digit), device_id_type=MESH,
        )

    def reduce_arrived(stage, pair, digit):
        axis = REDUCE_AXES[pair][stage]
        pltpu.make_async_remote_copy(
            src_ref=outs[stage].at[pair, digit], dst_ref=boxes[stage].at[pair, digit],
            send_sem=red_send.at[stage, pair, digit], recv_sem=red_recv.at[stage, pair, digit],
            device_id=peer(axis, digit), device_id_type=MESH,
        ).wait_recv()

    @pl.loop(1, RING)
    def _(step):
        for pair in range(COLOURS):
            digit = turn(REDUCE_AXES[pair][0], step)
            mixed, stats = tile(pair, digit)
            out1[pair, digit, :, :128] = mixed
            out1[pair, digit, :, 128:] = stats
            reduce_copy(0, pair, digit).start()

    for pair in range(COLOURS):
        own = here[REDUCE_AXES[pair][0]]
        mixed, stats = tile(pair, own)
        box1[pair, own, :, :128] = mixed
        box1[pair, own, :, 128:] = stats

    for stage in (1, 2):
        for pair in range(COLOURS):
            for step in range(1, RING):
                reduce_arrived(stage - 1, pair, turn(REDUCE_AXES[pair][stage - 1], step))
            acc, top, total = merged(boxes[stage - 1][pair])
            joined = jnp.concatenate([acc.astype(BF16), packed_stats(top, total)], axis=1)
            axis = REDUCE_AXES[pair][stage]
            if stage == 1:
                joined = joined.reshape(RING, RING, each, 256)
                rest = [i for i in range(3) if i != REDUCE_AXES[pair][0]]
                pieces = [
                    (joined[i] if rest[0] == axis else joined[:, i]).reshape(RING * each, 256)
                    for i in range(RING)
                ]
            else:
                pieces = [joined[i * each : (i + 1) * each] for i in range(RING)]
            for i in range(RING):
                outs[stage][pair, i] = pieces[i]
            boxes[stage][pair, here[axis]] = outs[stage][pair, here[axis]]
            for step in range(1, RING):
                reduce_copy(stage, pair, turn(axis, step)).start()

    partial = jnp.zeros((each, D), F32)
    for pair in range(COLOURS):
        for step in range(1, RING):
            reduce_arrived(2, pair, turn(REDUCE_AXES[pair][2], step))
        acc, _, total = merged(box3[pair])
        partial += dot((acc / total).astype(BF16), wo[pair * 128 : (pair + 1) * 128, :])
    mine[...] = partial
    swap = pltpu.make_async_remote_copy(
        src_ref=mine, dst_ref=theirs, send_sem=pair_send.at[4], recv_sem=pair_recv.at[4],
        device_id=partner, device_id_type=MESH,
    )
    swap.start()
    swap.wait()
    before = hidden[pl.ds(pl.multiple_of(cell * each, each), each), :].astype(F32) + (mine[...] + theirs[...])
    square = jnp.mean(before * before, axis=-1, keepdims=True)
    normal = (before * lax.rsqrt(square + EPS) * gain[...].reshape(1, D)).astype(BF16)
    for colour in range(COLOURS):
        block = normal[:, colour * 256 : (colour + 1) * 256]
        latents[2 * colour + core, here[0], here[1], here[2]] = jnp.where(core == 0, block[:, :128], block[:, 128:])

    def slab(colour, side, stage, axis=None, digit=None):
        known = GATHER_AXES[colour][stage:]
        at = [here[i] if i in known else slice(None) for i in range(3)]
        if axis is not None:
            at[axis] = digit
        return latents.at[(2 * colour + side,) + tuple(at)]

    def gather_copy(stage, colour, digit):
        axis = GATHER_AXES[colour][stage]
        return pltpu.make_async_remote_copy(
            src_ref=slab(colour, core, stage), dst_ref=slab(colour, core, stage),
            send_sem=gat_send.at[stage, colour, digit], recv_sem=gat_recv.at[stage, colour, here[axis]],
            device_id=peer(axis, digit), device_id_type=MESH,
        )

    def gather_arrived(stage, colour, digit):
        axis = GATHER_AXES[colour][stage]
        pltpu.make_async_remote_copy(
            src_ref=slab(colour, core, stage), dst_ref=slab(colour, core, stage, axis, digit),
            send_sem=gat_send.at[stage, colour, digit], recv_sem=gat_recv.at[stage, colour, digit],
            device_id=peer(axis, digit), device_id_type=MESH,
        ).wait_recv()

    def forward(colour, side, digit):
        axis = GATHER_AXES[colour][2]
        part = slab(colour, side, 2, axis, digit)
        return pltpu.make_async_remote_copy(
            src_ref=part, dst_ref=part, send_sem=fwd_send.at[colour, digit], recv_sem=fwd_recv.at[colour, digit],
            device_id=partner, device_id_type=MESH,
        )

    for stage in range(3):
        for colour in range(COLOURS):
            if stage:
                for step in range(1, RING):
                    gather_arrived(stage - 1, colour, turn(GATHER_AXES[colour][stage - 1], step))
            axis = GATHER_AXES[colour][stage]
            for step in range(1, RING):
                gather_copy(stage, colour, turn(axis, step)).start()
            if stage == 2:
                forward(colour, core, here[axis]).start()
    for step in (1, 3, 2):
        for colour in range(COLOURS):
            digit = turn(GATHER_AXES[colour][2], step)
            gather_arrived(2, colour, digit)
            forward(colour, core, digit).start()
    for colour in range(COLOURS):
        for digit in range(RING):
            forward(colour, 1 - core, digit).wait_recv()
    for colour in range(COLOURS):
        for digit in range(RING):
            forward(colour, core, digit).wait_send()
        for stage in range(3):
            for step in range(1, RING):
                reduce_copy(stage, colour, turn(REDUCE_AXES[colour][stage], step)).wait_send()
                gather_copy(stage, colour, turn(GATHER_AXES[colour][stage], step)).wait_send()
    for copy in weights:
        copy.wait()


def decoder(lat, emb, tally, soft, q0, q1, k0, k1, v0, v1, o0, o1, latent_out, tokens, k_scr, v_scr, q_scr, a_scr):
    core = lax.axis_index("qgrp")
    blocks, rows, _ = lat.shape
    group = q0.shape[1]
    slots = tokens.shape[0]
    pairs = group // 128
    own = pl.ds(pl.multiple_of(core * slots, slots), slots)
    latent = jnp.concatenate([lat[i] for i in range(blocks)], axis=1)
    latent_out[...] = latent.astype(F32)
    low = lanes((1, group)) % 128 < HD
    for side, (wq, wk, wv) in enumerate(((q0, k0, v0), (q1, k1, v1))):
        at = slice(side * group, (side + 1) * group)
        q_scr[:, at] = dot(emb[own, :], wq[...]).astype(BF16)
        keys = dot(latent, wk[...])
        k_scr[0, :, at] = jnp.where(low, keys, 0.0).astype(BF16)
        k_scr[1, :, at] = jnp.where(low, 0.0, keys).astype(BF16)
        values = dot(latent, wv[...]).astype(BF16)
        for pair in range(pairs):
            v_scr[side * pairs + pair, :, :128] = values[:, pair * 128 : (pair + 1) * 128]
            v_scr[side * pairs + pair, :, 128:] = jnp.ones((rows, 128), BF16)

    @pl.loop(0, 2 * pairs)
    def _(pair):
        at = pl.ds(pl.multiple_of(pair * 128, 128), 128)
        side = lax.rem(core + pair // pairs, 2)
        first = side * (2 * pairs) + 2 * lax.rem(pair, pairs)
        halves = []
        for part in range(2):
            scale = soft[1, first + part] * HD**-0.5
            scores = dot_nt(q_scr[:, at], k_scr[part, :, at])
            top = jnp.max(scores, axis=-1, keepdims=True)
            weights = jnp.exp2((scores - top) * (scale * LOG2E)).astype(BF16)
            mixed = dot(weights, v_scr[pair])
            halves.append(mixed[:, :128] / mixed[:, 128:])
        a_scr[:, at] = jnp.where(lanes((slots, 128)) < HD, halves[0], halves[1]).astype(BF16)

    update = dot(a_scr[:, :group], o0[...]) + dot(a_scr[:, group:], o1[...])
    position = core * slots + lax.broadcasted_iota(jnp.int32, (slots, 1), 0)
    tokens[...] = jnp.where(position < tally[0], emb[own, :].astype(F32) + update, 0.0)


def body(emb, tally, hidden, soft, gq, gk, gv, go, uq, uk, uv, uo, gain):
    rows, group = hidden.shape[0], gq.shape[1]
    slots = emb.shape[0]
    each = rows // RING**3
    dma = pltpu.SemaphoreType.DMA
    like = lambda x: jax.ShapeDtypeStruct(x.shape, x.dtype)
    boxes = []
    for part in (rows // RING, rows // RING**2, each):
        boxes += [pltpu.VMEM((COLOURS, RING, part, 256), BF16)] * 2
    latents, tq, tk, tv, to = pl.pallas_call(
        gather,
        name="gather",
        out_shape=(
            jax.ShapeDtypeStruct((2 * COLOURS, RING, RING, RING, each, 128), BF16),
            like(uq), like(uk), like(uv), like(uo),
        ),
        in_specs=[VMEM, SMEM, VMEM, SMEM, VMEM, VMEM, VMEM, VMEM, VMEM, ANY, ANY, ANY, ANY],
        out_specs=(VMEM, ANY, ANY, ANY, ANY),
        scratch_shapes=[
            pltpu.VMEM((COLOURS, RING, RING, RING, each, 128), BF16),
            pltpu.VMEM((2, slots, group), BF16),
            pltpu.VMEM((COLOURS, slots, 256), BF16),
            *boxes,
            pltpu.VMEM((each, D), F32),
            pltpu.VMEM((each, D), F32),
            dma((3, COLOURS, RING)), dma((3, COLOURS, RING)),
            dma((3, COLOURS, RING)), dma((3, COLOURS, RING)),
            dma((COLOURS, RING)), dma((COLOURS, RING)), dma((5,)), dma((5,)),
        ],
        compiler_params=pltpu.CompilerParams(collective_id=0, has_side_effects=True, vmem_limit_bytes=LIMIT),
    )(emb, tally, hidden, soft, gq, gk, gv, go, gain, uq, uk, uv, uo)
    half = slots // 2
    return pl.pallas_call(
        decoder,
        name="decoder",
        out_shape=(jax.ShapeDtypeStruct((rows, D), F32), jax.ShapeDtypeStruct((half, D), F32)),
        in_specs=[VMEM, VMEM, SMEM, SMEM] + [VMEM] * 8,
        out_specs=(VMEM, VMEM),
        scratch_shapes=[
            pltpu.VMEM((2, rows, D), BF16),
            pltpu.VMEM((2 * COLOURS, rows, 256), BF16),
            pltpu.VMEM((half, D), BF16),
            pltpu.VMEM((half, D), BF16),
        ],
        compiler_params=pltpu.CompilerParams(vmem_limit_bytes=LIMIT),
    )(latents.reshape(2 * COLOURS, rows, 128), emb, tally, soft, uq, tq, uk, tk, uv, tv, uo, to)


def solution(mesh):
    column, row = P(None, "qgrp"), P("qgrp", None)
    placed = (P("cell", None), P("cell"), P(), P(), column, column, column, row, column, column, column, row, P())
    return jax.shard_map(
        body,
        mesh=mesh,
        in_specs=placed,
        out_specs=(P(), P(("cell", "qgrp"), None)),
        check_vma=False,
    )
```

```python
import functools
import math

import jax
import jax.numpy as jnp
from jax import lax
from jax.experimental import pallas as pl
from jax.experimental.pallas import tpu as pltpu
from jax.sharding import PartitionSpec as P

D = 768
HEADS = 12
HD = 64
RING = 4
COLOURS = 3
REDUCE_AXES = ((0, 1, 2), (1, 2, 0), (2, 0, 1))
GATHER_AXES = ((2, 1, 0), (0, 2, 1), (1, 0, 2))
MASKED = -1e30
EPS = 1e-06
LOG2E = math.log2(math.e)
MESH = pl.DeviceIdType.MESH
F32 = jnp.float32
BF16 = jnp.bfloat16
VMEM = pl.BlockSpec(memory_space=pltpu.VMEM)
SMEM = pl.BlockSpec(memory_space=pltpu.SMEM)
HBM = pl.BlockSpec(memory_space=pltpu.HBM)
LIMIT = 36 * 1024 * 1024


def dot(a, b):
    return jnp.dot(a, b, preferred_element_type=F32)


def dot_nt(a, b):
    return lax.dot_general(a, b, (((1,), (1,)), ((), ())), preferred_element_type=F32)


def lanes(shape):
    return lax.broadcasted_iota(jnp.int32, shape, len(shape) - 1)


def three(x):
    high = x.astype(BF16).astype(F32)
    rest = x - high
    middle = rest.astype(BF16).astype(F32)
    return high, middle, rest - middle


def packed_stats(top, total):
    place = lanes(top.shape) % HD
    packed = jnp.zeros_like(top)
    for i, part in enumerate(three(top) + three(total)):
        packed = jnp.where(place == i, part, packed)
    return packed.astype(BF16)


def unpacking():
    source = lax.broadcasted_iota(jnp.int32, (128, 256), 0)
    target = lanes((128, 256))
    same = (target % 128) // HD == source // HD
    return (same & ((source % HD) // 3 == target // 128)).astype(BF16)


def merged(box):
    count, rows, _ = box.shape
    stats = dot(box[:, :, 128:].reshape(count * rows, 128), unpacking()).reshape(count, rows, 256)
    top, total = stats[:, :, :128], stats[:, :, 128:]
    best = jnp.max(top, axis=0)
    factor = jnp.exp(top - best)
    return jnp.sum(factor * box[:, :, :128].astype(F32), axis=0), best, jnp.sum(factor * total, axis=0)


def attend(q, k, v, scales):
    first = lanes((1, 128)) < HD
    zero = jnp.zeros_like(k)
    halves = (jnp.where(first, k, zero), jnp.where(first, zero, k))
    widened = jnp.concatenate([v, jnp.ones_like(v)], axis=1)
    tile, results = 128, []
    for start in range(0, q.shape[0], tile):
        mixed = []
        for key, scale in zip(halves, scales):
            scores = dot_nt(q[start : start + tile], key)
            top = jnp.max(scores, axis=-1, keepdims=True)
            weight = jnp.exp2((scores - top) * (scale * LOG2E)).astype(BF16)
            both = dot(weight, widened)
            mixed.append(both[:, :128] / both[:, 128:])
        results.append(jnp.where(first, mixed[0], mixed[1]).astype(BF16))
    return jnp.concatenate(results, axis=0)


def gather(
    emb_h, tally, hidden_h, soft_h, wq_h, wk_h, wv_h, wo_h, gain_h, dq_h, dk_h, dv_h, do_h,
    latents, att, q_other, k_other, v_other, o_other,
    emb, hidden, soft, wq, wk, wv, wo, gain, dq, dk, dv, dq_other, q_own, k_own, v_own,
    q_scr, k_scr, v_scr, out1, box1, out2, box2, out3, box3, mine, theirs,
    load_sem, red_send, red_recv, gat_send, gat_recv, fwd_send, fwd_recv, pair_send, pair_recv,
):
    cell, core = lax.axis_index("cell"), lax.axis_index("qgrp")
    here = (cell // 16, (cell // 4) % 4, cell % 4)
    partner = (cell, 1 - core)
    rows, group = hidden.shape[0], wq.shape[1]
    slots = emb.shape[0]
    quarter, each = rows // RING, rows // RING**3
    loads = {}
    for i, (name, source, target) in enumerate((
        ("emb", emb_h, emb), ("wk", wk_h, wk), ("wv", wv_h, wv), ("hidden", hidden_h, hidden), ("wq", wq_h, wq),
        ("soft", soft_h, soft), ("dq", dq_h, dq), ("wo", wo_h, wo), ("gain", gain_h, gain),
        ("dk", dk_h, dk), ("dv", dv_h, dv),
    )):
        loads[name] = pltpu.make_async_copy(source, target, load_sem.at[i])
        loads[name].start()

    def ready(*names):
        for name in names:
            loads[name].wait()

    def peer(axis, digit):
        at = [digit if i == axis else here[i] for i in range(3)]
        return ((at[0] * RING + at[1]) * RING + at[2], core)

    def turn(axis, step):
        return lax.rem(here[axis] + step, RING)

    def to_partner(i, source, target):
        return pltpu.make_async_remote_copy(
            src_ref=source, dst_ref=target, send_sem=pair_send.at[i], recv_sem=pair_recv.at[i],
            device_id=partner, device_id_type=MESH,
        )

    barrier = pltpu.get_barrier_semaphore()
    for axis in range(3):
        for step in range(1, RING):
            pl.semaphore_signal(barrier, inc=1, device_id=peer(axis, turn(axis, step)), device_id_type=MESH)
    pl.semaphore_signal(barrier, inc=1, device_id=partner, device_id_type=MESH)

    ready("emb", "wk")
    keys = dot(emb[...], wk[...])
    low = lanes((1, group)) % 128 < HD
    k_scr[0] = jnp.where(low, keys, 0.0).astype(BF16)
    k_scr[1] = jnp.where(low, 0.0, keys).astype(BF16)
    ready("wv")
    values = dot(emb[...], wv[...]).astype(BF16)
    for pair in range(COLOURS):
        v_scr[pair, :, :128] = values[:, pair * 128 : (pair + 1) * 128]
        v_scr[pair, :, 128:] = jnp.ones((slots, 128), BF16)
    ready("hidden", "wq")
    queries = dot(hidden[...], wq[...]).astype(BF16)
    for pair in range(COLOURS):
        q_scr[pair] = queries[:, pair * 128 : (pair + 1) * 128].reshape(RING, RING, RING, each, 128)
    bias = jnp.where(lanes((1, slots)) < tally[0], 0.0, MASKED)
    first_head = core * (2 * COLOURS)
    ready("soft")

    pl.semaphore_wait(barrier, 10)
    swaps = [to_partner(0, dq_h, dq_other), to_partner(1, do_h, o_other)]
    for copy in swaps:
        copy.start()

    def tile(pair, digit):
        axis = REDUCE_AXES[pair][0]
        q = q_scr[(pair,) + tuple(digit if i == axis else slice(None) for i in range(axis + 1))]
        q = q.reshape(quarter, 128)
        first = lanes((quarter, 128)) < HD
        tops, halves = [], []
        for part in range(2):
            scale = soft[0, first_head + 2 * pair + part] * HD**-0.5
            scores = dot_nt(q, k_scr[part, :, pair * 128 : (pair + 1) * 128]) + bias
            top = jnp.max(scores, axis=-1, keepdims=True)
            weight = jnp.exp2((scores - top) * (scale * LOG2E)).astype(BF16)
            halves.append(dot(weight, v_scr[pair]))
            tops.append(top * scale)
        mixed = jnp.where(first, halves[0][:, :128], halves[1][:, :128])
        total = jnp.where(first, halves[0][:, 128:], halves[1][:, 128:])
        return mixed.astype(BF16), packed_stats(jnp.where(first, tops[0], tops[1]), total)

    outs, boxes = (out1, out2, out3), (box1, box2, box3)

    def reduce_copy(stage, pair, digit):
        axis = REDUCE_AXES[pair][stage]
        return pltpu.make_async_remote_copy(
            src_ref=outs[stage].at[pair, digit], dst_ref=boxes[stage].at[pair, here[axis]],
            send_sem=red_send.at[stage, pair, digit], recv_sem=red_recv.at[stage, pair, here[axis]],
            device_id=peer(axis, digit), device_id_type=MESH,
        )

    def reduce_arrived(stage, pair, digit):
        axis = REDUCE_AXES[pair][stage]
        pltpu.make_async_remote_copy(
            src_ref=outs[stage].at[pair, digit], dst_ref=boxes[stage].at[pair, digit],
            send_sem=red_send.at[stage, pair, digit], recv_sem=red_recv.at[stage, pair, digit],
            device_id=peer(axis, digit), device_id_type=MESH,
        ).wait_recv()

    @pl.loop(1, RING)
    def _(step):
        for pair in range(COLOURS):
            digit = turn(REDUCE_AXES[pair][0], step)
            mixed, stats = tile(pair, digit)
            out1[pair, digit, :, :128] = mixed
            out1[pair, digit, :, 128:] = stats
            reduce_copy(0, pair, digit).start()

    for pair in range(COLOURS):
        own = here[REDUCE_AXES[pair][0]]
        mixed, stats = tile(pair, own)
        box1[pair, own, :, :128] = mixed
        box1[pair, own, :, 128:] = stats

    half = slots // 2
    ready("dq", "wo", "gain", "dk", "dv")
    mine_rows = emb[pl.ds(pl.multiple_of(core * half, half), half), :]
    for target, weight in ((q_own, dq), (q_other, dq_other)):
        if weight is dq_other:
            for copy in swaps:
                copy.wait()
        projected = dot(mine_rows, weight[...]).astype(BF16)
        for pair in range(COLOURS):
            target[pair] = projected[:, pair * 128 : (pair + 1) * 128]

    for stage in (1, 2):
        for pair in range(COLOURS):
            for step in range(1, RING):
                reduce_arrived(stage - 1, pair, turn(REDUCE_AXES[pair][stage - 1], step))
            acc, top, total = merged(boxes[stage - 1][pair])
            joined = jnp.concatenate([acc.astype(BF16), packed_stats(top, total)], axis=1)
            axis = REDUCE_AXES[pair][stage]
            if stage == 1:
                joined = joined.reshape(RING, RING, each, 256)
                rest = [i for i in range(3) if i != REDUCE_AXES[pair][0]]
                pieces = [
                    (joined[i] if rest[0] == axis else joined[:, i]).reshape(RING * each, 256)
                    for i in range(RING)
                ]
            else:
                pieces = [joined[i * each : (i + 1) * each] for i in range(RING)]
            for i in range(RING):
                outs[stage][pair, i] = pieces[i]
            boxes[stage][pair, here[axis]] = outs[stage][pair, here[axis]]
            for step in range(1, RING):
                reduce_copy(stage, pair, turn(axis, step)).start()

    partial = jnp.zeros((each, D), F32)
    for pair in range(COLOURS):
        for step in range(1, RING):
            reduce_arrived(2, pair, turn(REDUCE_AXES[pair][2], step))
        acc, _, total = merged(box3[pair])
        partial += dot((acc / total).astype(BF16), wo[pair * 128 : (pair + 1) * 128, :])
    mine[...] = partial
    swap = to_partner(2, mine, theirs)
    swap.start()
    swap.wait()
    before = hidden[pl.ds(pl.multiple_of(cell * each, each), each), :].astype(F32) + (mine[...] + theirs[...])
    square = jnp.mean(before * before, axis=-1, keepdims=True)
    normal = (before * lax.rsqrt(square + EPS) * gain[...].reshape(1, D)).astype(BF16)
    for colour in range(COLOURS):
        block = normal[:, colour * 256 : (colour + 1) * 256]
        latents[2 * colour + core, here[0], here[1], here[2]] = jnp.where(core == 0, block[:, :128], block[:, 128:])

    def slab(colour, side, stage, axis=None, digit=None):
        known = GATHER_AXES[colour][stage:]
        at = [here[i] if i in known else slice(None) for i in range(3)]
        if axis is not None:
            at[axis] = digit
        return latents.at[(2 * colour + side,) + tuple(at)]

    def gather_copy(stage, colour, digit):
        axis = GATHER_AXES[colour][stage]
        return pltpu.make_async_remote_copy(
            src_ref=slab(colour, core, stage), dst_ref=slab(colour, core, stage),
            send_sem=gat_send.at[stage, colour, digit], recv_sem=gat_recv.at[stage, colour, here[axis]],
            device_id=peer(axis, digit), device_id_type=MESH,
        )

    def gather_arrived(stage, colour, digit):
        axis = GATHER_AXES[colour][stage]
        pltpu.make_async_remote_copy(
            src_ref=slab(colour, core, stage), dst_ref=slab(colour, core, stage, axis, digit),
            send_sem=gat_send.at[stage, colour, digit], recv_sem=gat_recv.at[stage, colour, digit],
            device_id=peer(axis, digit), device_id_type=MESH,
        ).wait_recv()

    def forward(colour, side, digit):
        axis = GATHER_AXES[colour][2]
        part = slab(colour, side, 2, axis, digit)
        return pltpu.make_async_remote_copy(
            src_ref=part, dst_ref=part, send_sem=fwd_send.at[colour, digit], recv_sem=fwd_recv.at[colour, digit],
            device_id=partner, device_id_type=MESH,
        )

    for stage in range(3):
        for colour in range(COLOURS):
            if stage:
                for step in range(1, RING):
                    gather_arrived(stage - 1, colour, turn(GATHER_AXES[colour][stage - 1], step))
            axis = GATHER_AXES[colour][stage]
            for step in range(1, RING):
                gather_copy(stage, colour, turn(axis, step)).start()
            if stage == 2:
                forward(colour, core, here[axis]).start()
    for step in (1, 3, 2):
        for colour in range(COLOURS):
            digit = turn(GATHER_AXES[colour][2], step)
            gather_arrived(2, colour, digit)
            forward(colour, core, digit).start()
    for colour in range(COLOURS):
        for digit in range(RING):
            forward(colour, 1 - core, digit).wait_recv()
    latent = jnp.concatenate([latents[i].reshape(rows, 128) for i in range(2 * COLOURS)], axis=1)
    shares = []
    for i, (own, weight, target) in enumerate(((k_own, dk, k_other), (v_own, dv, v_other))):
        projected = dot(latent, weight[...]).astype(BF16)
        for pair in range(COLOURS):
            own[pair] = projected[:, pair * 128 : (pair + 1) * 128]
        shares.append(to_partner(3 + i, own, target))
        shares[-1].start()

    @pl.loop(0, COLOURS)
    def _(pair):
        scales = [soft[1, first_head + 2 * pair + part] * HD**-0.5 for part in range(2)]
        att[pair] = attend(q_own[pair], k_own[pair], v_own[pair], scales)

    for colour in range(COLOURS):
        for digit in range(RING):
            forward(colour, core, digit).wait_send()
        for stage in range(3):
            for step in range(1, RING):
                reduce_copy(stage, colour, turn(REDUCE_AXES[colour][stage], step)).wait_send()
                gather_copy(stage, colour, turn(GATHER_AXES[colour][stage], step)).wait_send()
    for copy in shares:
        copy.wait()


def decoder(
    lat, att, q, k, v, o_other, emb_h, tally, soft_h, o_own_h,
    latent_out, tokens, emb, soft, o_own, wide, other, sem,
):
    core = lax.axis_index("qgrp")
    blocks, rows, _ = lat.shape
    slots, pairs = q.shape[1], q.shape[0]
    loads = [
        pltpu.make_async_copy(soft_h, soft, sem.at[0]),
        pltpu.make_async_copy(emb_h.at[pl.ds(pl.multiple_of(core * slots, slots), slots)], emb, sem.at[1]),
        pltpu.make_async_copy(o_own_h, o_own, sem.at[2]),
    ]
    for copy in loads:
        copy.start()
    for i in range(blocks):
        wide[:, i * 128 : (i + 1) * 128] = lat[i].astype(F32)
    write = pltpu.make_async_copy(wide, latent_out, sem.at[3])
    write.start()
    loads[0].wait()
    first = (1 - core) * (2 * pairs)

    @pl.loop(0, pairs)
    def _(pair):
        scales = [soft[1, first + 2 * pair + part] * HD**-0.5 for part in range(2)]
        other[pair] = attend(q[pair], k[pair], v[pair], scales)

    for copy in loads[1:]:
        copy.wait()
    own_att = jnp.concatenate([att[i] for i in range(pairs)], axis=1)
    other_att = jnp.concatenate([other[i] for i in range(pairs)], axis=1)
    update = dot(own_att, o_own[...]) + dot(other_att, o_other[...])
    position = core * slots + lax.broadcasted_iota(jnp.int32, (slots, 1), 0)
    tokens[...] = jnp.where(position < tally[0], emb[...].astype(F32) + update, 0.0)
    write.wait()


def body(emb, tally, hidden, soft, gq, gk, gv, go, uq, uk, uv, uo, gain):
    rows, group = hidden.shape[0], gq.shape[1]
    slots = emb.shape[0]
    half = slots // 2
    each = rows // RING**3
    dma = pltpu.SemaphoreType.DMA
    held = lambda x: pltpu.VMEM(x.shape, x.dtype)
    emb, hidden, soft, gq, gk, gv, go, uq, uk, uv, uo, gain = (
        pltpu.with_memory_space_constraint(x, pltpu.HBM)
        for x in (emb, hidden, soft, gq, gk, gv, go, uq, uk, uv, uo, gain)
    )
    boxes = []
    for part in (rows // RING, rows // RING**2, each):
        boxes += [pltpu.VMEM((COLOURS, RING, part, 256), BF16)] * 2
    latents, att, q, k, v, o_other = pl.pallas_call(
        gather,
        name="gather",
        out_shape=(
            jax.ShapeDtypeStruct((2 * COLOURS, RING, RING, RING, each, 128), BF16),
            jax.ShapeDtypeStruct((COLOURS, half, 128), BF16),
            jax.ShapeDtypeStruct((COLOURS, half, 128), BF16),
            jax.ShapeDtypeStruct((COLOURS, rows, 128), BF16),
            jax.ShapeDtypeStruct((COLOURS, rows, 128), BF16),
            jax.ShapeDtypeStruct(uo.shape, BF16),
        ),
        in_specs=[HBM, SMEM] + [HBM] * 11,
        out_specs=(VMEM,) * 6,
        scratch_shapes=[
            held(emb), held(hidden), pltpu.SMEM(soft.shape, F32), held(gq), held(gk), held(gv), held(go), held(gain),
            held(uq), held(uk), held(uv), held(uq),
            pltpu.VMEM((COLOURS, half, 128), BF16),
            pltpu.VMEM((COLOURS, rows, 128), BF16),
            pltpu.VMEM((COLOURS, rows, 128), BF16),
            pltpu.VMEM((COLOURS, RING, RING, RING, each, 128), BF16),
            pltpu.VMEM((2, slots, group), BF16),
            pltpu.VMEM((COLOURS, slots, 256), BF16),
            *boxes,
            pltpu.VMEM((each, D), F32),
            pltpu.VMEM((each, D), F32),
            dma((11,)), dma((3, COLOURS, RING)), dma((3, COLOURS, RING)),
            dma((3, COLOURS, RING)), dma((3, COLOURS, RING)),
            dma((COLOURS, RING)), dma((COLOURS, RING)), dma((5,)), dma((5,)),
        ],
        compiler_params=pltpu.CompilerParams(collective_id=0, has_side_effects=True, vmem_limit_bytes=LIMIT),
    )(emb, tally, hidden, soft, gq, gk, gv, go, gain, uq, uk, uv, uo)
    return pl.pallas_call(
        decoder,
        name="decoder",
        out_shape=(jax.ShapeDtypeStruct((rows, D), F32), jax.ShapeDtypeStruct((half, D), F32)),
        in_specs=[VMEM] * 6 + [HBM, SMEM, HBM, HBM],
        out_specs=(HBM, VMEM),
        scratch_shapes=[
            pltpu.VMEM((half, D), BF16), pltpu.SMEM(soft.shape, F32), held(uo), pltpu.VMEM((rows, D), F32),
            pltpu.VMEM((COLOURS, half, 128), BF16), dma((4,)),
        ],
        compiler_params=pltpu.CompilerParams(vmem_limit_bytes=LIMIT),
    )(latents.reshape(2 * COLOURS, rows, 128), att, q, k, v, o_other, emb, tally, soft, uo)


def solution(mesh):
    column, row = P(None, "qgrp"), P("qgrp", None)
    placed = (P("cell", None), P("cell"), P(), P(), column, column, column, row, column, column, column, row, P())
    return jax.shard_map(
        body,
        mesh=mesh,
        in_specs=placed,
        out_specs=(P(), P(("cell", "qgrp"), None)),
        check_vma=False,
    )
```

```python
import functools
import math

import jax
import jax.numpy as jnp
from jax import lax
from jax.experimental import pallas as pl
from jax.experimental.pallas import tpu as pltpu
from jax.sharding import PartitionSpec as P

D = 768
HEADS = 12
HD = 64
RING = 4
COLOURS = 3
REDUCE_AXES = ((0, 1, 2), (1, 2, 0), (2, 0, 1))
GATHER_AXES = ((2, 1, 0), (0, 2, 1), (1, 0, 2))
MASKED = -1e30
EPS = 1e-06
LOG2E = math.log2(math.e)
MESH = pl.DeviceIdType.MESH
F32 = jnp.float32
BF16 = jnp.bfloat16
VMEM = pl.BlockSpec(memory_space=pltpu.VMEM)
SMEM = pl.BlockSpec(memory_space=pltpu.SMEM)
HBM = pl.BlockSpec(memory_space=pltpu.HBM)
LIMIT = 36 * 1024 * 1024


def dot(a, b):
    return jnp.dot(a, b, preferred_element_type=F32)


def dot_nt(a, b):
    return lax.dot_general(a, b, (((1,), (1,)), ((), ())), preferred_element_type=F32)


def lanes(shape):
    return lax.broadcasted_iota(jnp.int32, shape, len(shape) - 1)


def three(x):
    high = x.astype(BF16).astype(F32)
    rest = x - high
    middle = rest.astype(BF16).astype(F32)
    return high, middle, rest - middle


def columns(rows):
    width = rows.shape[1]
    held = jnp.concatenate([rows, jnp.zeros((14, width), F32)], axis=0).astype(BF16)
    head = lax.broadcasted_iota(jnp.int32, (16, 128), 0)
    spread = (lanes((16, 128)) // HD == head).astype(BF16)
    return lax.dot_general(held, spread, (((0,), (0,)), ((), ())), preferred_element_type=F32)


def merged(accs, stats):
    rows = accs.shape[1]
    best = functools.reduce(jnp.maximum, [stats[i, 0:2] for i in range(RING)])
    acc, total = 0.0, 0.0
    for i in range(RING):
        factor = jnp.exp2(stats[i, 0:2] - best).astype(BF16).astype(F32)
        total += factor * stats[i, 2:4]
        acc += columns(factor)[:rows] * accs[i].astype(F32)
    return acc, best, total


def attend(q, k, v, scales):
    first = lanes((1, 128)) < HD
    zero = jnp.zeros_like(k)
    halves = (jnp.where(first, k, zero), jnp.where(first, zero, k))
    widened = jnp.concatenate([v, jnp.ones_like(v)], axis=1)
    tile, results = 128, []
    for start in range(0, q.shape[0], tile):
        mixed = []
        for key, scale in zip(halves, scales):
            scores = dot_nt(q[start : start + tile], key)
            top = jnp.max(scores, axis=-1, keepdims=True)
            weight = jnp.exp2((scores - top) * (scale * LOG2E)).astype(BF16)
            both = dot(weight, widened)
            mixed.append(both[:, :128] / both[:, 128:])
        results.append(jnp.where(first, mixed[0], mixed[1]).astype(BF16))
    return jnp.concatenate(results, axis=0)


def gather(
    emb_h, tally, hidden_h, soft_h, wq_h, wk_h, wv_h, wo_h, gain_h, dq_h, dk_h, dv_h, do_h,
    latents, att, q_other, k_other, v_other, o_other,
    emb, hidden, soft, wq, wk, wv, wo, gain, dq, dk, dv, dq_other, q_own, k_own, v_own,
    q_scr, k_scr, v_scr, *rest,
):
    outs = (rest[0:2], rest[4:6], rest[8:10])
    boxes = (rest[2:4], rest[6:8], rest[10:12])
    mine, theirs, load_sem, red_send, red_recv, gat_send, gat_recv, fwd_send, fwd_recv, pair_send, pair_recv = rest[12:]
    cell, core = lax.axis_index("cell"), lax.axis_index("qgrp")
    here = (cell // 16, (cell // 4) % 4, cell % 4)
    partner = (cell, 1 - core)
    rows, group = hidden.shape[0], wq.shape[1]
    slots = emb.shape[0]
    quarter, each = rows // RING, rows // RING**3
    loads = {}
    for i, (name, source, target) in enumerate((
        ("emb", emb_h, emb), ("wk", wk_h, wk), ("wv", wv_h, wv), ("hidden", hidden_h, hidden), ("wq", wq_h, wq),
        ("soft", soft_h, soft), ("dq", dq_h, dq), ("wo", wo_h, wo), ("gain", gain_h, gain),
        ("dk", dk_h, dk), ("dv", dv_h, dv),
    )):
        loads[name] = pltpu.make_async_copy(source, target, load_sem.at[i])
        loads[name].start()

    def ready(*names):
        for name in names:
            loads[name].wait()

    def peer(axis, digit):
        at = [digit if i == axis else here[i] for i in range(3)]
        return ((at[0] * RING + at[1]) * RING + at[2], core)

    def turn(axis, step):
        return lax.rem(here[axis] + step, RING)

    def to_partner(i, source, target):
        return pltpu.make_async_remote_copy(
            src_ref=source, dst_ref=target, send_sem=pair_send.at[i], recv_sem=pair_recv.at[i],
            device_id=partner, device_id_type=MESH,
        )

    barrier = pltpu.get_barrier_semaphore()
    for axis in range(3):
        for step in range(1, RING):
            pl.semaphore_signal(barrier, inc=1, device_id=peer(axis, turn(axis, step)), device_id_type=MESH)
    pl.semaphore_signal(barrier, inc=1, device_id=partner, device_id_type=MESH)

    first_head = core * (2 * COLOURS)
    first = lanes((1, 128)) < HD
    valid = lax.broadcasted_iota(jnp.int32, (slots, 1), 0) < tally[0]
    ready("emb", "wk", "soft")
    keys = dot(emb[...], wk[...]).astype(BF16).astype(F32)
    keys = jnp.where(valid, keys, keys[0:1])
    for pair in range(COLOURS):
        scale = [soft[0, first_head + 2 * pair + part] * (HD**-0.5 * LOG2E) for part in range(2)]
        scaled = keys[:, pair * 128 : (pair + 1) * 128] * jnp.where(first, scale[0], scale[1])
        high = scaled.astype(BF16).astype(F32)
        rest = scaled - high
        k_scr[2 * pair] = jnp.where(first, high, pltpu.roll(rest, HD, 1)).astype(BF16)
        k_scr[2 * pair + 1] = jnp.where(first, pltpu.roll(high, HD, 1), rest).astype(BF16)
    ready("wv")
    values = jnp.where(valid, dot(emb[...], wv[...]), 0.0).astype(BF16)
    for pair in range(COLOURS):
        v_scr[pair, :, :128] = values[:, pair * 128 : (pair + 1) * 128]
        v_scr[pair, :, 128:] = jnp.broadcast_to(jnp.where(valid, 1.0, 0.0), (slots, 128)).astype(BF16)
    ready("hidden", "wq")
    queries = dot(hidden[...], wq[...])
    for pair in range(COLOURS):
        one = queries[:, pair * 128 : (pair + 1) * 128]
        other = pltpu.roll(one, HD, 1)
        for part in range(2):
            double = jnp.where(first == (part == 0), one, other).astype(BF16)
            q_scr[2 * pair + part] = double.reshape(RING, RING, RING, each, 128)

    pl.semaphore_wait(barrier, 10)
    swaps = [to_partner(0, dq_h, dq_other), to_partner(1, do_h, o_other)]
    for copy in swaps:
        copy.start()

    def tile(pair, digit):
        axis, following, _ = REDUCE_AXES[pair]
        rest = [i for i in range(3) if i != axis]
        where = tuple(digit if i == axis else slice(None) for i in range(axis + 1))
        tops, both = [], []
        for part in range(2):
            q = q_scr[(2 * pair + part,) + where]
            if rest[0] != following:
                q = jnp.concatenate([q[:, i].reshape(RING * each, 128) for i in range(RING)], axis=0)
            scores = dot_nt(q.reshape(quarter, 128), k_scr[2 * pair + part])
            tops.append(jnp.max(scores, axis=-1, keepdims=True))
            both.append(dot(jnp.exp2(scores - tops[-1]).astype(BF16), v_scr[pair]))
        acc = jnp.where(first, both[0][:, :128], both[1][:, :128]).astype(BF16)
        lane = lanes((1, 128))
        stats = jnp.where(lane == 0, tops[0], jnp.where(lane == 1, tops[1], jnp.where(lane == 2, both[0][:, 128:], both[1][:, 128:])))
        return acc, stats.T[0:8]

    def reduce_copy(stage, pair, digit):
        axis = REDUCE_AXES[pair][stage]
        return [
            pltpu.make_async_remote_copy(
                src_ref=outs[stage][i].at[pair, digit], dst_ref=boxes[stage][i].at[pair, here[axis]],
                send_sem=red_send.at[stage, pair, digit, i], recv_sem=red_recv.at[stage, pair, here[axis], i],
                device_id=peer(axis, digit), device_id_type=MESH,
            )
            for i in range(2)
        ]

    def reduce_arrived(stage, pair, digit):
        axis = REDUCE_AXES[pair][stage]
        for i in range(2):
            pltpu.make_async_remote_copy(
                src_ref=outs[stage][i].at[pair, digit], dst_ref=boxes[stage][i].at[pair, digit],
                send_sem=red_send.at[stage, pair, digit, i], recv_sem=red_recv.at[stage, pair, digit, i],
                device_id=peer(axis, digit), device_id_type=MESH,
            ).wait_recv()

    @pl.loop(0, RING - 1)
    def _(i):
        step = lax.rem(2 + i + i * (i - 1) // 2, RING)
        digits = [turn(REDUCE_AXES[pair][0], step) for pair in range(COLOURS)]
        for pair in range(COLOURS):
            outs[0][0][pair, digits[pair]], outs[0][1][pair, digits[pair]] = tile(pair, digits[pair])
        for pair in range(COLOURS):
            for copy in reduce_copy(0, pair, digits[pair]):
                copy.start()

    for pair in range(COLOURS):
        own = here[REDUCE_AXES[pair][0]]
        boxes[0][0][pair, own], boxes[0][1][pair, own] = tile(pair, own)

    half = slots // 2
    ready("dq", "wo", "gain", "dk", "dv")
    mine_rows = emb[pl.ds(pl.multiple_of(core * half, half), half), :]
    for target, weight in ((q_own, dq), (q_other, dq_other)):
        if weight is dq_other:
            for copy in swaps:
                copy.wait()
        projected = dot(mine_rows, weight[...]).astype(BF16)
        for pair in range(COLOURS):
            target[pair] = projected[:, pair * 128 : (pair + 1) * 128]

    for stage in (1, 2):
        for pair in range(COLOURS):
            for step in range(1, RING):
                reduce_arrived(stage - 1, pair, turn(REDUCE_AXES[pair][stage - 1], step))
        part = rows // RING ** (stage + 1)
        for pair in range(COLOURS):
            acc, top, total = merged(*(box.at[pair] for box in boxes[stage - 1]))
            stats = jnp.concatenate([top, total, jnp.zeros((4, top.shape[1]), F32)], axis=0)
            for i in range(RING):
                outs[stage][0][pair, i] = acc[i * part : (i + 1) * part].astype(BF16)
                outs[stage][1][pair, i] = jnp.concatenate(
                    [stats[:, i * part : (i + 1) * part], jnp.zeros((8, 128 - part), F32)], axis=1
                )
        for pair in range(COLOURS):
            axis = REDUCE_AXES[pair][stage]
            for step in (2, 1, 3):
                for copy in reduce_copy(stage, pair, turn(axis, step)):
                    copy.start()
        for pair in range(COLOURS):
            own = here[REDUCE_AXES[pair][stage]]
            for i in range(2):
                boxes[stage][i][pair, own] = outs[stage][i][pair, own]

    for pair in range(COLOURS):
        for step in range(1, RING):
            reduce_arrived(2, pair, turn(REDUCE_AXES[pair][2], step))
    partial = jnp.zeros((each, D), F32)
    for pair in range(COLOURS):
        acc, _, total = merged(*(box.at[pair] for box in boxes[2]))
        inverse = sum(columns(x)[:each] for x in three(1.0 / jnp.where(lanes(total.shape) < each, total, 1.0)))
        partial += dot((acc * inverse).astype(BF16), wo[pair * 128 : (pair + 1) * 128, :])
    mine[...] = partial
    swap = to_partner(2, mine, theirs)
    swap.start()
    swap.wait()
    before = hidden[pl.ds(pl.multiple_of(cell * each, each), each), :].astype(F32) + (mine[...] + theirs[...])
    square = jnp.mean(before * before, axis=-1, keepdims=True)
    normal = (before * lax.rsqrt(square + EPS) * gain[...].reshape(1, D)).astype(BF16)
    for colour in range(COLOURS):
        block = normal[:, colour * 256 : (colour + 1) * 256]
        latents[2 * colour + core, here[0], here[1], here[2]] = jnp.where(core == 0, block[:, :128], block[:, 128:])

    def slab(colour, side, stage, axis=None, digit=None):
        known = GATHER_AXES[colour][stage:]
        at = [here[i] if i in known else slice(None) for i in range(3)]
        if axis is not None:
            at[axis] = digit
        return latents.at[(2 * colour + side,) + tuple(at)]

    def gather_copy(stage, colour, digit):
        axis = GATHER_AXES[colour][stage]
        return pltpu.make_async_remote_copy(
            src_ref=slab(colour, core, stage), dst_ref=slab(colour, core, stage),
            send_sem=gat_send.at[stage, colour, digit], recv_sem=gat_recv.at[stage, colour, here[axis]],
            device_id=peer(axis, digit), device_id_type=MESH,
        )

    def gather_arrived(stage, colour, digit):
        axis = GATHER_AXES[colour][stage]
        pltpu.make_async_remote_copy(
            src_ref=slab(colour, core, stage), dst_ref=slab(colour, core, stage, axis, digit),
            send_sem=gat_send.at[stage, colour, digit], recv_sem=gat_recv.at[stage, colour, digit],
            device_id=peer(axis, digit), device_id_type=MESH,
        ).wait_recv()

    def forward(colour, side, digit):
        axis = GATHER_AXES[colour][2]
        part = slab(colour, side, 2, axis, digit)
        return pltpu.make_async_remote_copy(
            src_ref=part, dst_ref=part, send_sem=fwd_send.at[colour, digit], recv_sem=fwd_recv.at[colour, digit],
            device_id=partner, device_id_type=MESH,
        )

    for stage in range(3):
        for colour in range(COLOURS):
            if stage:
                for step in range(1, RING):
                    gather_arrived(stage - 1, colour, turn(GATHER_AXES[colour][stage - 1], step))
            axis = GATHER_AXES[colour][stage]
            for step in range(1, RING):
                gather_copy(stage, colour, turn(axis, step)).start()
            if stage == 2:
                forward(colour, core, here[axis]).start()
    for step in (1, 3, 2):
        for colour in range(COLOURS):
            digit = turn(GATHER_AXES[colour][2], step)
            gather_arrived(2, colour, digit)
            forward(colour, core, digit).start()
    for colour in range(COLOURS):
        for digit in range(RING):
            forward(colour, 1 - core, digit).wait_recv()
    latent = jnp.concatenate([latents[i].reshape(rows, 128) for i in range(2 * COLOURS)], axis=1)
    shares = []
    for i, (own, weight, target) in enumerate(((k_own, dk, k_other), (v_own, dv, v_other))):
        projected = dot(latent, weight[...]).astype(BF16)
        for pair in range(COLOURS):
            own[pair] = projected[:, pair * 128 : (pair + 1) * 128]
        shares.append(to_partner(3 + i, own, target))
        shares[-1].start()

    for pair in range(COLOURS):
        scales = [soft[1, first_head + 2 * pair + part] * HD**-0.5 for part in range(2)]
        att[pair] = attend(q_own[pair], k_own[pair], v_own[pair], scales)

    for colour in range(COLOURS):
        for digit in range(RING):
            forward(colour, core, digit).wait_send()
        for stage in range(3):
            for step in range(1, RING):
                for copy in reduce_copy(stage, colour, turn(REDUCE_AXES[colour][stage], step)):
                    copy.wait_send()
                gather_copy(stage, colour, turn(GATHER_AXES[colour][stage], step)).wait_send()
    for copy in shares:
        copy.wait()


def decoder(
    lat, att, q, k, v, o_other, emb_h, tally, soft_h, o_own_h,
    latent_out, tokens, emb, soft, o_own, wide, other, sem,
):
    core = lax.axis_index("qgrp")
    blocks, rows, _ = lat.shape
    slots, pairs = q.shape[1], q.shape[0]
    loads = [
        pltpu.make_async_copy(soft_h, soft, sem.at[0]),
        pltpu.make_async_copy(emb_h.at[pl.ds(pl.multiple_of(core * slots, slots), slots)], emb, sem.at[1]),
        pltpu.make_async_copy(o_own_h, o_own, sem.at[2]),
    ]
    for copy in loads:
        copy.start()
    for i in range(blocks):
        wide[:, i * 128 : (i + 1) * 128] = lat[i].astype(F32)
    write = pltpu.make_async_copy(wide, latent_out, sem.at[3])
    write.start()
    loads[0].wait()
    first = (1 - core) * (2 * pairs)

    for pair in range(pairs):
        scales = [soft[1, first + 2 * pair + part] * HD**-0.5 for part in range(2)]
        other[pair] = attend(q[pair], k[pair], v[pair], scales)

    for copy in loads[1:]:
        copy.wait()
    own_att = jnp.concatenate([att[i] for i in range(pairs)], axis=1)
    other_att = jnp.concatenate([other[i] for i in range(pairs)], axis=1)
    update = dot(own_att, o_own[...]) + dot(other_att, o_other[...])
    position = core * slots + lax.broadcasted_iota(jnp.int32, (slots, 1), 0)
    tokens[...] = jnp.where(position < tally[0], emb[...].astype(F32) + update, 0.0)
    write.wait()


def body(emb, tally, hidden, soft, gq, gk, gv, go, uq, uk, uv, uo, gain):
    rows, group = hidden.shape[0], gq.shape[1]
    slots = emb.shape[0]
    half = slots // 2
    each = rows // RING**3
    dma = pltpu.SemaphoreType.DMA
    held = lambda x: pltpu.VMEM(x.shape, x.dtype)
    emb, hidden, soft, gq, gk, gv, go, uq, uk, uv, uo, gain = (
        pltpu.with_memory_space_constraint(x, pltpu.HBM)
        for x in (emb, hidden, soft, gq, gk, gv, go, uq, uk, uv, uo, gain)
    )
    boxes = []
    for part in (rows // RING, rows // RING**2, each):
        boxes += [
            pltpu.VMEM((COLOURS, RING, part, 128), BF16),
            pltpu.VMEM((COLOURS, RING, 8, max(part, 128)), F32),
        ] * 2
    latents, att, q, k, v, o_other = pl.pallas_call(
        gather,
        name="gather",
        out_shape=(
            jax.ShapeDtypeStruct((2 * COLOURS, RING, RING, RING, each, 128), BF16),
            jax.ShapeDtypeStruct((COLOURS, half, 128), BF16),
            jax.ShapeDtypeStruct((COLOURS, half, 128), BF16),
            jax.ShapeDtypeStruct((COLOURS, rows, 128), BF16),
            jax.ShapeDtypeStruct((COLOURS, rows, 128), BF16),
            jax.ShapeDtypeStruct(uo.shape, BF16),
        ),
        in_specs=[HBM, SMEM] + [HBM] * 11,
        out_specs=(VMEM,) * 6,
        scratch_shapes=[
            held(emb), held(hidden), pltpu.SMEM(soft.shape, F32), held(gq), held(gk), held(gv), held(go), held(gain),
            held(uq), held(uk), held(uv), held(uq),
            pltpu.VMEM((COLOURS, half, 128), BF16),
            pltpu.VMEM((COLOURS, rows, 128), BF16),
            pltpu.VMEM((COLOURS, rows, 128), BF16),
            pltpu.VMEM((2 * COLOURS, RING, RING, RING, each, 128), BF16),
            pltpu.VMEM((2 * COLOURS, slots, 128), BF16),
            pltpu.VMEM((COLOURS, slots, 256), BF16),
            *boxes,
            pltpu.VMEM((each, D), F32),
            pltpu.VMEM((each, D), F32),
            dma((11,)), dma((3, COLOURS, RING, 2)), dma((3, COLOURS, RING, 2)),
            dma((3, COLOURS, RING)), dma((3, COLOURS, RING)),
            dma((COLOURS, RING)), dma((COLOURS, RING)), dma((5,)), dma((5,)),
        ],
        compiler_params=pltpu.CompilerParams(collective_id=0, has_side_effects=True, vmem_limit_bytes=LIMIT),
    )(emb, tally, hidden, soft, gq, gk, gv, go, gain, uq, uk, uv, uo)
    return pl.pallas_call(
        decoder,
        name="decoder",
        out_shape=(jax.ShapeDtypeStruct((rows, D), F32), jax.ShapeDtypeStruct((half, D), F32)),
        in_specs=[VMEM] * 6 + [HBM, SMEM, HBM, HBM],
        out_specs=(HBM, VMEM),
        scratch_shapes=[
            pltpu.VMEM((half, D), BF16), pltpu.SMEM(soft.shape, F32), held(uo), pltpu.VMEM((rows, D), F32),
            pltpu.VMEM((COLOURS, half, 128), BF16), dma((4,)),
        ],
        compiler_params=pltpu.CompilerParams(vmem_limit_bytes=LIMIT),
    )(latents.reshape(2 * COLOURS, rows, 128), att, q, k, v, o_other, emb, tally, soft, uo)


def solution(mesh):
    column, row = P(None, "qgrp"), P("qgrp", None)
    placed = (P("cell", None), P("cell"), P(), P(), column, column, column, row, column, column, column, row, P())
    return jax.shard_map(
        body,
        mesh=mesh,
        in_specs=placed,
        out_specs=(P(), P(("cell", "qgrp"), None)),
        check_vma=False,
    )
```

```python
import functools
import math

import jax
import jax.numpy as jnp
from jax import lax
from jax.experimental import pallas as pl
from jax.experimental.pallas import tpu as pltpu
from jax.sharding import PartitionSpec as P

D = 768
HEADS = 12
HD = 64
RING = 4
COLOURS = 3
REDUCE_AXES = ((0, 1, 2), (1, 2, 0), (2, 0, 1))
GATHER_AXES = ((2, 1, 0), (0, 2, 1), (1, 0, 2))
MASKED = -1e30
EPS = 1e-06
LOG2E = math.log2(math.e)
MESH = pl.DeviceIdType.MESH
F32 = jnp.float32
BF16 = jnp.bfloat16
VMEM = pl.BlockSpec(memory_space=pltpu.VMEM)
SMEM = pl.BlockSpec(memory_space=pltpu.SMEM)
HBM = pl.BlockSpec(memory_space=pltpu.HBM)
LIMIT = 36 * 1024 * 1024


def dot(a, b):
    return jnp.dot(a, b, preferred_element_type=F32)


def dot_nt(a, b):
    return lax.dot_general(a, b, (((1,), (1,)), ((), ())), preferred_element_type=F32)


def lanes(shape):
    return lax.broadcasted_iota(jnp.int32, shape, len(shape) - 1)


def three(x):
    high = x.astype(BF16).astype(F32)
    rest = x - high
    middle = rest.astype(BF16).astype(F32)
    return high, middle, rest - middle


def columns(rows):
    width = rows.shape[1]
    held = jnp.concatenate([rows, jnp.zeros((14, width), F32)], axis=0).astype(BF16)
    head = lax.broadcasted_iota(jnp.int32, (16, 128), 0)
    spread = (lanes((16, 128)) // HD == head).astype(BF16)
    return lax.dot_general(held, spread, (((0,), (0,)), ((), ())), preferred_element_type=F32)


def merged(accs, stats):
    rows = accs.shape[1]
    best = functools.reduce(jnp.maximum, [stats[i, 0:2] for i in range(RING)])
    acc, total = 0.0, 0.0
    for i in range(RING):
        factor = jnp.exp2(stats[i, 0:2] - best).astype(BF16).astype(F32)
        total += factor * stats[i, 2:4]
        acc += columns(factor)[:rows] * accs[i].astype(F32)
    return acc, best, total


def attend(q, k, v, scales):
    first = lanes((1, 128)) < HD
    zero = jnp.zeros_like(k)
    halves = (jnp.where(first, k, zero), jnp.where(first, zero, k))
    widened = jnp.concatenate([v, jnp.ones_like(v)], axis=1)
    tile, results = 128, []
    for start in range(0, q.shape[0], tile):
        mixed = []
        for key, scale in zip(halves, scales):
            scores = dot_nt(q[start : start + tile], key)
            top = jnp.max(scores, axis=-1, keepdims=True)
            weight = jnp.exp2((scores - top) * (scale * LOG2E)).astype(BF16)
            both = dot(weight, widened)
            mixed.append(both[:, :128] / both[:, 128:])
        results.append(jnp.where(first, mixed[0], mixed[1]).astype(BF16))
    return jnp.concatenate(results, axis=0)


def gather(
    emb_h, tally, hidden_h, soft_h, wq_h, wk_h, wv_h, wo_h, gain_h, dq_h, dk_h, dv_h, do_h,
    latents, att, att_other, o_other,
    emb, hidden, soft, wq, wk, wv, wo, gain, dq, dk, dv, q_own, k_own, v_own, att_send,
    q_scr, k_scr, v_scr, *rest,
):
    outs = (rest[0:2], rest[4:6], rest[8:10])
    boxes = (rest[2:4], rest[6:8], rest[10:12])
    mine, theirs, load_sem, red_send, red_recv, gat_send, gat_recv, last_recv, fwd_send, fwd_recv, pair_send, pair_recv = rest[12:]
    cell, core = lax.axis_index("cell"), lax.axis_index("qgrp")
    here = (cell // 16, (cell // 4) % 4, cell % 4)
    partner = (cell, 1 - core)
    rows, group = hidden.shape[0], wq.shape[1]
    slots = emb.shape[0]
    quarter, each = rows // RING, rows // RING**3
    loads = {}
    for i, (name, source, target) in enumerate((
        ("emb", emb_h, emb), ("wk", wk_h, wk), ("wv", wv_h, wv), ("hidden", hidden_h, hidden), ("wq", wq_h, wq),
        ("soft", soft_h, soft), ("dq", dq_h, dq), ("wo", wo_h, wo), ("gain", gain_h, gain),
        ("dk", dk_h, dk), ("dv", dv_h, dv),
    )):
        loads[name] = pltpu.make_async_copy(source, target, load_sem.at[i])
        loads[name].start()

    def ready(*names):
        for name in names:
            loads[name].wait()

    def peer(axis, digit):
        at = [digit if i == axis else here[i] for i in range(3)]
        return ((at[0] * RING + at[1]) * RING + at[2], core)

    def turn(axis, step):
        return lax.rem(here[axis] + step, RING)

    def to_partner(i, source, target):
        return pltpu.make_async_remote_copy(
            src_ref=source, dst_ref=target, send_sem=pair_send.at[i], recv_sem=pair_recv.at[i],
            device_id=partner, device_id_type=MESH,
        )

    barrier = pltpu.get_barrier_semaphore()
    for axis in range(3):
        for step in range(1, RING):
            pl.semaphore_signal(barrier, inc=1, device_id=peer(axis, turn(axis, step)), device_id_type=MESH)
    pl.semaphore_signal(barrier, inc=1, device_id=partner, device_id_type=MESH)

    first_head = core * (2 * COLOURS)
    first = lanes((1, 128)) < HD
    valid = lax.broadcasted_iota(jnp.int32, (slots, 1), 0) < tally[0]
    ready("emb", "wk", "soft", "wv")
    keys = dot(emb[...], wk[...]).astype(BF16).astype(F32)
    keys = jnp.where(valid, keys, keys[0:1])
    for pair in range(COLOURS):
        scale = [soft[0, first_head + 2 * pair + part] * (HD**-0.5 * LOG2E) for part in range(2)]
        scaled = keys[:, pair * 128 : (pair + 1) * 128] * jnp.where(first, scale[0], scale[1])
        high = scaled.astype(BF16).astype(F32)
        rest = scaled - high
        k_scr[2 * pair] = jnp.where(first, high, pltpu.roll(rest, HD, 1)).astype(BF16)
        k_scr[2 * pair + 1] = jnp.where(first, pltpu.roll(high, HD, 1), rest).astype(BF16)
    values = jnp.where(valid, dot(emb[...], wv[...]), 0.0).astype(BF16)
    for pair in range(COLOURS):
        v_scr[pair, :, :128] = values[:, pair * 128 : (pair + 1) * 128]
        v_scr[pair, :, 128:] = jnp.broadcast_to(jnp.where(valid, 1.0, 0.0), (slots, 128)).astype(BF16)
    ready("hidden", "wq")
    queries = dot(hidden[...], wq[...])
    for pair in range(COLOURS):
        one = queries[:, pair * 128 : (pair + 1) * 128]
        other = pltpu.roll(one, HD, 1)
        for part in range(2):
            double = jnp.where(first == (part == 0), one, other).astype(BF16)
            q_scr[2 * pair + part] = double.reshape(RING, RING, RING, each, 128)

    pl.semaphore_wait(barrier, 10)
    trade = to_partner(0, do_h, o_other)
    trade.start()

    def tile(pair, digit):
        axis, following, _ = REDUCE_AXES[pair]
        rest = [i for i in range(3) if i != axis]
        where = tuple(digit if i == axis else slice(None) for i in range(axis + 1))
        tops, both = [], []
        for part in range(2):
            q = q_scr[(2 * pair + part,) + where]
            if rest[0] != following:
                q = jnp.concatenate([q[:, i].reshape(RING * each, 128) for i in range(RING)], axis=0)
            scores = dot_nt(q.reshape(quarter, 128), k_scr[2 * pair + part])
            tops.append(jnp.max(scores, axis=-1, keepdims=True))
            both.append(dot(jnp.exp2(scores - tops[-1]).astype(BF16), v_scr[pair]))
        acc = jnp.where(first, both[0][:, :128], both[1][:, :128]).astype(BF16)
        lane = lanes((1, 128))
        stats = jnp.where(lane == 0, tops[0], jnp.where(lane == 1, tops[1], jnp.where(lane == 2, both[0][:, 128:], both[1][:, 128:])))
        return acc, stats.T[0:8]

    def reduce_copy(stage, pair, digit):
        axis = REDUCE_AXES[pair][stage]
        return [
            pltpu.make_async_remote_copy(
                src_ref=outs[stage][i].at[pair, digit], dst_ref=boxes[stage][i].at[pair, here[axis]],
                send_sem=red_send.at[stage, i], recv_sem=red_recv.at[stage, i],
                device_id=peer(axis, digit), device_id_type=MESH,
            )
            for i in range(2)
        ]

    def reduce_all(stage):
        return [
            pltpu.make_async_remote_copy(
                src_ref=outs[stage][i].at[:, pl.ds(0, RING - 1)], dst_ref=boxes[stage][i].at[:, pl.ds(0, RING - 1)],
                send_sem=red_send.at[stage, i], recv_sem=red_recv.at[stage, i],
                device_id=partner, device_id_type=MESH,
            )
            for i in range(2)
        ]

    @pl.loop(0, RING - 1)
    def _(i):
        step = lax.rem(2 + i + i * (i - 1) // 2, RING)
        digits = [turn(REDUCE_AXES[pair][0], step) for pair in range(COLOURS)]
        for pair in range(COLOURS):
            outs[0][0][pair, digits[pair]], outs[0][1][pair, digits[pair]] = tile(pair, digits[pair])
        for pair in range(COLOURS):
            for copy in reduce_copy(0, pair, digits[pair]):
                copy.start()

    for pair in range(COLOURS):
        own = here[REDUCE_AXES[pair][0]]
        boxes[0][0][pair, own], boxes[0][1][pair, own] = tile(pair, own)

    half = slots // 2
    ready("dq", "wo", "gain", "dk", "dv")
    projected = dot(emb[...], dq[...]).astype(BF16)
    for pair in range(COLOURS):
        q_own[pair] = projected[:, pair * 128 : (pair + 1) * 128]

    for stage in (1, 2):
        for copy in reduce_all(stage - 1):
            copy.wait_recv()
        part = rows // RING ** (stage + 1)
        for pair in range(COLOURS):
            acc, top, total = merged(*(box.at[pair] for box in boxes[stage - 1]))
            stats = jnp.concatenate([top, total, jnp.zeros((4, top.shape[1]), F32)], axis=0)
            for i in range(RING):
                outs[stage][0][pair, i] = acc[i * part : (i + 1) * part].astype(BF16)
                outs[stage][1][pair, i] = jnp.concatenate(
                    [stats[:, i * part : (i + 1) * part], jnp.zeros((8, 128 - part), F32)], axis=1
                )
        for pair in range(COLOURS):
            axis = REDUCE_AXES[pair][stage]
            for step in (2, 1, 3):
                for copy in reduce_copy(stage, pair, turn(axis, step)):
                    copy.start()
        for pair in range(COLOURS):
            own = here[REDUCE_AXES[pair][stage]]
            for i in range(2):
                boxes[stage][i][pair, own] = outs[stage][i][pair, own]

    for copy in reduce_all(2):
        copy.wait_recv()
    partial = jnp.zeros((each, D), F32)
    for pair in range(COLOURS):
        acc, _, total = merged(*(box.at[pair] for box in boxes[2]))
        inverse = sum(columns(x)[:each] for x in three(1.0 / jnp.where(lanes(total.shape) < each, total, 1.0)))
        partial += dot((acc * inverse).astype(BF16), wo[pair * 128 : (pair + 1) * 128, :])
    mine[...] = partial
    swap = to_partner(2, mine, theirs)
    swap.start()
    swap.wait()
    before = hidden[pl.ds(pl.multiple_of(cell * each, each), each), :].astype(F32) + (mine[...] + theirs[...])
    square = jnp.mean(before * before, axis=-1, keepdims=True)
    normal = (before * lax.rsqrt(square + EPS) * gain[...].reshape(1, D)).astype(BF16)
    for colour in range(COLOURS):
        block = normal[:, colour * 256 : (colour + 1) * 256]
        latents[2 * colour + core, here[0], here[1], here[2]] = jnp.where(core == 0, block[:, :128], block[:, 128:])

    def slab(colour, side, stage, axis=None, digit=None):
        known = GATHER_AXES[colour][stage:]
        at = [here[i] if i in known else slice(None) for i in range(3)]
        if axis is not None:
            at[axis] = digit
        return latents.at[(2 * colour + side,) + tuple(at)]

    def gather_copy(stage, colour, digit):
        axis = GATHER_AXES[colour][stage]
        arrival = last_recv.at[colour, here[axis]] if stage == 2 else gat_recv.at[stage, colour]
        return pltpu.make_async_remote_copy(
            src_ref=slab(colour, core, stage), dst_ref=slab(colour, core, stage),
            send_sem=gat_send.at[stage, colour], recv_sem=arrival,
            device_id=peer(axis, digit), device_id_type=MESH,
        )

    def gather_all(stage, colour):
        part = latents.at[(2 * colour + core,) + (0,) * (2 - stage) + (pl.ds(0, RING - 1),)]
        return pltpu.make_async_remote_copy(
            src_ref=part, dst_ref=part, send_sem=gat_send.at[stage, colour],
            recv_sem=gat_recv.at[min(stage, 1), colour], device_id=partner, device_id_type=MESH,
        )

    def gather_last(colour, digit):
        axis = GATHER_AXES[colour][2]
        return pltpu.make_async_remote_copy(
            src_ref=slab(colour, core, 2), dst_ref=slab(colour, core, 2, axis, digit),
            send_sem=gat_send.at[2, colour], recv_sem=last_recv.at[colour, digit],
            device_id=peer(axis, digit), device_id_type=MESH,
        )

    def forward(colour, part):
        return pltpu.make_async_remote_copy(
            src_ref=part, dst_ref=part, send_sem=fwd_send.at[colour], recv_sem=fwd_recv.at[colour],
            device_id=partner, device_id_type=MESH,
        )

    for stage in range(3):
        for colour in range(COLOURS):
            if stage:
                gather_all(stage - 1, colour).wait_recv()
            axis = GATHER_AXES[colour][stage]
            for step in (2, 1, 3):
                gather_copy(stage, colour, turn(axis, step)).start()
            if stage == 2:
                forward(colour, slab(colour, core, 2)).start()
        for copy in reduce_all(stage):
            copy.wait_send()
    for step in (1, 3, 2):
        for colour in range(COLOURS):
            axis = GATHER_AXES[colour][2]
            digit = turn(axis, step)
            gather_last(colour, digit).wait_recv()
            forward(colour, slab(colour, core, 2, axis, digit)).start()
    for stage in range(2):
        for colour in range(COLOURS):
            gather_all(stage, colour).wait_send()
    for colour in range(COLOURS):
        forward(colour, latents.at[2 * colour + 1 - core]).wait_recv()
    latent = jnp.concatenate([latents[i].reshape(rows, 128) for i in range(2 * COLOURS)], axis=1)
    for own, weight in ((k_own, dk), (v_own, dv)):
        projected = dot(latent, weight[...]).astype(BF16)
        for pair in range(COLOURS):
            own[pair] = projected[:, pair * 128 : (pair + 1) * 128]

    def attended(pair, side):
        q = q_own[pair, pl.ds(pl.multiple_of(side * half, half), half)]
        scales = [soft[1, first_head + 2 * pair + part] * HD**-0.5 for part in range(2)]
        return attend(q, k_own[pair], v_own[pair], scales)

    shares = [to_partner(i, att_send.at[pair], att_other.at[pair]) for pair, i in enumerate((1, 3, 4))]
    for pair in range(COLOURS):
        att_send[pair] = attended(pair, 1 - core)
    for copy in shares:
        copy.start()
    for pair in range(COLOURS):
        att[pair] = attended(pair, core)

    for colour in range(COLOURS):
        forward(colour, latents.at[2 * colour + core]).wait_send()
        gather_all(2, colour).wait_send()
    trade.wait()
    for copy in shares:
        copy.wait()


def decoder(
    lat, att, att_other, o_other, emb_h, tally, o_own_h,
    latent_out, tokens, emb, o_own, wide, sem,
):
    core = lax.axis_index("qgrp")
    blocks = lat.shape[0]
    pairs, slots, _ = att.shape
    loads = [
        pltpu.make_async_copy(emb_h.at[pl.ds(pl.multiple_of(core * slots, slots), slots)], emb, sem.at[0]),
        pltpu.make_async_copy(o_own_h, o_own, sem.at[1]),
    ]
    for copy in loads:
        copy.start()
    for i in range(blocks):
        wide[:, i * 128 : (i + 1) * 128] = lat[i].astype(F32)
    write = pltpu.make_async_copy(wide, latent_out, sem.at[2])
    write.start()
    for copy in loads:
        copy.wait()
    own = jnp.concatenate([att[i] for i in range(pairs)], axis=1)
    other = jnp.concatenate([att_other[i] for i in range(pairs)], axis=1)
    update = dot(own, o_own[...]) + dot(other, o_other[...])
    position = core * slots + lax.broadcasted_iota(jnp.int32, (slots, 1), 0)
    tokens[...] = jnp.where(position < tally[0], emb[...].astype(F32) + update, 0.0)
    write.wait()


def body(emb, tally, hidden, soft, gq, gk, gv, go, uq, uk, uv, uo, gain):
    rows, group = hidden.shape[0], gq.shape[1]
    slots = emb.shape[0]
    half = slots // 2
    each = rows // RING**3
    dma = pltpu.SemaphoreType.DMA
    held = lambda x: pltpu.VMEM(x.shape, x.dtype)
    emb, hidden, soft, gq, gk, gv, go, uq, uk, uv, uo, gain = (
        pltpu.with_memory_space_constraint(x, pltpu.HBM)
        for x in (emb, hidden, soft, gq, gk, gv, go, uq, uk, uv, uo, gain)
    )
    boxes = []
    for part in (rows // RING, rows // RING**2, each):
        boxes += [
            pltpu.VMEM((COLOURS, RING, part, 128), BF16),
            pltpu.VMEM((COLOURS, RING, 8, max(part, 128)), F32),
        ] * 2
    latents, att, att_other, o_other = pl.pallas_call(
        gather,
        name="gather",
        out_shape=(
            jax.ShapeDtypeStruct((2 * COLOURS, RING, RING, RING, each, 128), BF16),
            jax.ShapeDtypeStruct((COLOURS, half, 128), BF16),
            jax.ShapeDtypeStruct((COLOURS, half, 128), BF16),
            jax.ShapeDtypeStruct(uo.shape, BF16),
        ),
        in_specs=[HBM, SMEM] + [HBM] * 11,
        out_specs=(VMEM,) * 4,
        scratch_shapes=[
            held(emb), held(hidden), pltpu.SMEM(soft.shape, F32), held(gq), held(gk), held(gv), held(go), held(gain),
            held(uq), held(uk), held(uv),
            pltpu.VMEM((COLOURS, slots, 128), BF16),
            pltpu.VMEM((COLOURS, rows, 128), BF16),
            pltpu.VMEM((COLOURS, rows, 128), BF16),
            pltpu.VMEM((COLOURS, half, 128), BF16),
            pltpu.VMEM((2 * COLOURS, RING, RING, RING, each, 128), BF16),
            pltpu.VMEM((2 * COLOURS, slots, 128), BF16),
            pltpu.VMEM((COLOURS, slots, 256), BF16),
            *boxes,
            pltpu.VMEM((each, D), F32),
            pltpu.VMEM((each, D), F32),
            dma((11,)), dma((3, 2)), dma((3, 2)), dma((3, COLOURS)), dma((2, COLOURS)), dma((COLOURS, RING)),
            dma((COLOURS,)), dma((COLOURS,)), dma((5,)), dma((5,)),
        ],
        compiler_params=pltpu.CompilerParams(collective_id=0, has_side_effects=True, vmem_limit_bytes=LIMIT),
    )(emb, tally, hidden, soft, gq, gk, gv, go, gain, uq, uk, uv, uo)
    return pl.pallas_call(
        decoder,
        name="decoder",
        out_shape=(jax.ShapeDtypeStruct((rows, D), F32), jax.ShapeDtypeStruct((half, D), F32)),
        in_specs=[VMEM] * 4 + [HBM, SMEM, HBM],
        out_specs=(HBM, VMEM),
        scratch_shapes=[pltpu.VMEM((half, D), BF16), held(uo), pltpu.VMEM((rows, D), F32), dma((3,))],
        compiler_params=pltpu.CompilerParams(vmem_limit_bytes=LIMIT),
    )(latents.reshape(2 * COLOURS, rows, 128), att, att_other, o_other, emb, tally, uo)


def solution(mesh):
    column, row = P(None, "qgrp"), P("qgrp", None)
    placed = (P("cell", None), P("cell"), P(), P(), column, column, column, row, column, column, column, row, P())
    return jax.shard_map(
        body,
        mesh=mesh,
        in_specs=placed,
        out_specs=(P(), P(("cell", "qgrp"), None)),
        check_vma=False,
    )
```

```python
import functools
import math

import jax
import jax.numpy as jnp
from jax import lax
from jax.experimental import pallas as pl
from jax.experimental.pallas import tpu as pltpu
from jax.sharding import PartitionSpec as P

D = 768
HEADS = 12
HD = 64
RING = 4
COLOURS = 3
REDUCE_AXES = ((0, 1, 2), (1, 2, 0), (2, 0, 1))
GATHER_AXES = ((2, 1, 0), (0, 2, 1), (1, 0, 2))
MASKED = -1e30
EPS = 1e-06
LOG2E = math.log2(math.e)
MESH = pl.DeviceIdType.MESH
F32 = jnp.float32
BF16 = jnp.bfloat16
VMEM = pl.BlockSpec(memory_space=pltpu.VMEM)
SMEM = pl.BlockSpec(memory_space=pltpu.SMEM)
HBM = pl.BlockSpec(memory_space=pltpu.HBM)
LIMIT = 36 * 1024 * 1024


def dot(a, b):
    return jnp.dot(a, b, preferred_element_type=F32)


def dot_nt(a, b):
    return lax.dot_general(a, b, (((1,), (1,)), ((), ())), preferred_element_type=F32)


def lanes(shape):
    return lax.broadcasted_iota(jnp.int32, shape, len(shape) - 1)


def three(x):
    high = x.astype(BF16).astype(F32)
    rest = x - high
    middle = rest.astype(BF16).astype(F32)
    return high, middle, rest - middle


def columns(rows):
    width = rows.shape[1]
    held = jnp.concatenate([rows, jnp.zeros((14, width), F32)], axis=0).astype(BF16)
    head = lax.broadcasted_iota(jnp.int32, (16, 128), 0)
    spread = (lanes((16, 128)) // HD == head).astype(BF16)
    return lax.dot_general(held, spread, (((0,), (0,)), ((), ())), preferred_element_type=F32)


def merged(accs, stats):
    rows = accs.shape[1]
    best = functools.reduce(jnp.maximum, [stats[i, 0:2] for i in range(RING)])
    acc, total = 0.0, 0.0
    for i in range(RING):
        factor = jnp.exp2(stats[i, 0:2] - best).astype(BF16).astype(F32)
        total += factor * stats[i, 2:4]
        acc += columns(factor)[:rows] * accs[i].astype(F32)
    return acc, best, total


def attend(q, k, v, scales):
    first = lanes((1, 128)) < HD
    zero = jnp.zeros_like(k)
    halves = (jnp.where(first, k, zero), jnp.where(first, zero, k))
    widened = jnp.concatenate([v, jnp.ones_like(v)], axis=1)
    tile, results = 128, []
    for start in range(0, q.shape[0], tile):
        mixed = []
        for key, scale in zip(halves, scales):
            scores = dot_nt(q[start : start + tile], key)
            top = jnp.max(scores, axis=-1, keepdims=True)
            weight = jnp.exp2((scores - top) * (scale * LOG2E)).astype(BF16)
            both = dot(weight, widened)
            mixed.append(both[:, :128] / both[:, 128:])
        results.append(jnp.where(first, mixed[0], mixed[1]).astype(BF16))
    return jnp.concatenate(results, axis=0)


def gather(
    emb_h, tally, hidden_h, soft_h, wq_h, wk_h, wv_h, wo_h, gain_h, dq_h, dk_h, dv_h, do_h,
    wide, att, att_other, o_own, o_other, tokens,
    latents, emb, hidden, soft, wq, wk, wv, wo, gain, dq, dk, dv, q_own, k_own, v_own, att_send,
    q_scr, k_scr, v_scr, *rest,
):
    outs = (rest[0:2], rest[4:6], rest[8:10])
    boxes = (rest[2:4], rest[6:8], rest[10:12])
    mine, theirs, load_sem, red_send, red_recv, gat_send, gat_recv, last_recv, fwd_send, fwd_recv, pair_send, pair_recv = rest[12:]
    cell, core = lax.axis_index("cell"), lax.axis_index("qgrp")
    here = (cell // 16, (cell // 4) % 4, cell % 4)
    partner = (cell, 1 - core)
    rows, group = hidden.shape[0], wq.shape[1]
    slots = emb.shape[0]
    quarter, each = rows // RING, rows // RING**3
    loads = {}
    for i, (name, source, target) in enumerate((
        ("emb", emb_h, emb), ("wk", wk_h, wk), ("wv", wv_h, wv), ("hidden", hidden_h, hidden), ("wq", wq_h, wq),
        ("soft", soft_h, soft), ("dq", dq_h, dq), ("wo", wo_h, wo), ("gain", gain_h, gain),
        ("dk", dk_h, dk), ("dv", dv_h, dv), ("do", do_h, o_own),
    )):
        loads[name] = pltpu.make_async_copy(source, target, load_sem.at[i])
        loads[name].start()

    def ready(*names):
        for name in names:
            loads[name].wait()

    def peer(axis, digit):
        at = [digit if i == axis else here[i] for i in range(3)]
        return ((at[0] * RING + at[1]) * RING + at[2], core)

    def turn(axis, step):
        return lax.rem(here[axis] + step, RING)

    def to_partner(i, source, target):
        return pltpu.make_async_remote_copy(
            src_ref=source, dst_ref=target, send_sem=pair_send.at[i], recv_sem=pair_recv.at[i],
            device_id=partner, device_id_type=MESH,
        )

    barrier = pltpu.get_barrier_semaphore()
    for axis in range(3):
        for step in range(1, RING):
            pl.semaphore_signal(barrier, inc=1, device_id=peer(axis, turn(axis, step)), device_id_type=MESH)
    pl.semaphore_signal(barrier, inc=1, device_id=partner, device_id_type=MESH)

    first_head = core * (2 * COLOURS)
    first = lanes((1, 128)) < HD
    valid = lax.broadcasted_iota(jnp.int32, (slots, 1), 0) < tally[0]
    ready("emb", "wk", "soft", "wv")
    keys = dot(emb[...], wk[...]).astype(BF16).astype(F32)
    keys = jnp.where(valid, keys, keys[0:1])
    for pair in range(COLOURS):
        scale = [soft[0, first_head + 2 * pair + part] * (HD**-0.5 * LOG2E) for part in range(2)]
        scaled = keys[:, pair * 128 : (pair + 1) * 128] * jnp.where(first, scale[0], scale[1])
        high = scaled.astype(BF16).astype(F32)
        rest = scaled - high
        k_scr[2 * pair] = jnp.where(first, high, pltpu.roll(rest, HD, 1)).astype(BF16)
        k_scr[2 * pair + 1] = jnp.where(first, pltpu.roll(high, HD, 1), rest).astype(BF16)
    values = jnp.where(valid, dot(emb[...], wv[...]), 0.0).astype(BF16)
    for pair in range(COLOURS):
        v_scr[pair, :, :128] = values[:, pair * 128 : (pair + 1) * 128]
        v_scr[pair, :, 128:] = jnp.broadcast_to(jnp.where(valid, 1.0, 0.0), (slots, 128)).astype(BF16)
    ready("hidden", "wq")
    queries = dot(hidden[...], wq[...])
    for pair in range(COLOURS):
        one = queries[:, pair * 128 : (pair + 1) * 128]
        other = pltpu.roll(one, HD, 1)
        for part in range(2):
            double = jnp.where(first == (part == 0), one, other).astype(BF16)
            q_scr[2 * pair + part] = double.reshape(RING, RING, RING, each, 128)

    pl.semaphore_wait(barrier, 10)
    trade = to_partner(0, do_h, o_other)
    trade.start()

    def tile(pair, digit):
        axis, following, _ = REDUCE_AXES[pair]
        rest = [i for i in range(3) if i != axis]
        where = tuple(digit if i == axis else slice(None) for i in range(axis + 1))
        tops, both = [], []
        for part in range(2):
            q = q_scr[(2 * pair + part,) + where]
            if rest[0] != following:
                q = jnp.concatenate([q[:, i].reshape(RING * each, 128) for i in range(RING)], axis=0)
            scores = dot_nt(q.reshape(quarter, 128), k_scr[2 * pair + part])
            tops.append(jnp.max(scores, axis=-1, keepdims=True))
            both.append(dot(jnp.exp2(scores - tops[-1]).astype(BF16), v_scr[pair]))
        acc = jnp.where(first, both[0][:, :128], both[1][:, :128]).astype(BF16)
        lane = lanes((1, 128))
        stats = jnp.where(lane == 0, tops[0], jnp.where(lane == 1, tops[1], jnp.where(lane == 2, both[0][:, 128:], both[1][:, 128:])))
        return acc, stats.T[0:8]

    def reduce_copy(stage, pair, digit):
        axis = REDUCE_AXES[pair][stage]
        return [
            pltpu.make_async_remote_copy(
                src_ref=outs[stage][i].at[pair, digit], dst_ref=boxes[stage][i].at[pair, here[axis]],
                send_sem=red_send.at[stage, i], recv_sem=red_recv.at[stage, i],
                device_id=peer(axis, digit), device_id_type=MESH,
            )
            for i in range(2)
        ]

    def reduce_all(stage):
        return [
            pltpu.make_async_remote_copy(
                src_ref=outs[stage][i].at[:, pl.ds(0, RING - 1)], dst_ref=boxes[stage][i].at[:, pl.ds(0, RING - 1)],
                send_sem=red_send.at[stage, i], recv_sem=red_recv.at[stage, i],
                device_id=partner, device_id_type=MESH,
            )
            for i in range(2)
        ]

    @pl.loop(0, RING - 1)
    def _(i):
        step = lax.rem(2 + i + i * (i - 1) // 2, RING)
        digits = [turn(REDUCE_AXES[pair][0], step) for pair in range(COLOURS)]
        for pair in range(COLOURS):
            outs[0][0][pair, digits[pair]], outs[0][1][pair, digits[pair]] = tile(pair, digits[pair])
        for pair in range(COLOURS):
            for copy in reduce_copy(0, pair, digits[pair]):
                copy.start()

    for pair in range(COLOURS):
        own = here[REDUCE_AXES[pair][0]]
        boxes[0][0][pair, own], boxes[0][1][pair, own] = tile(pair, own)

    half = slots // 2
    ready("dq", "wo", "gain", "dk", "dv", "do")
    tokens[...] = emb[pl.ds(pl.multiple_of(core * half, half), half), :]
    projected = dot(emb[...], dq[...]).astype(BF16)
    for pair in range(COLOURS):
        q_own[pair] = projected[:, pair * 128 : (pair + 1) * 128]

    for stage in (1, 2):
        for copy in reduce_all(stage - 1):
            copy.wait_recv()
        part = rows // RING ** (stage + 1)
        for pair in range(COLOURS):
            acc, top, total = merged(*(box.at[pair] for box in boxes[stage - 1]))
            stats = jnp.concatenate([top, total, jnp.zeros((4, top.shape[1]), F32)], axis=0)
            for i in range(RING):
                outs[stage][0][pair, i] = acc[i * part : (i + 1) * part].astype(BF16)
                outs[stage][1][pair, i] = jnp.concatenate(
                    [stats[:, i * part : (i + 1) * part], jnp.zeros((8, 128 - part), F32)], axis=1
                )
        for pair in range(COLOURS):
            axis = REDUCE_AXES[pair][stage]
            for step in (2, 1, 3):
                for copy in reduce_copy(stage, pair, turn(axis, step)):
                    copy.start()
        for pair in range(COLOURS):
            own = here[REDUCE_AXES[pair][stage]]
            for i in range(2):
                boxes[stage][i][pair, own] = outs[stage][i][pair, own]

    for copy in reduce_all(2):
        copy.wait_recv()
    partial = jnp.zeros((each, D), F32)
    for pair in range(COLOURS):
        acc, _, total = merged(*(box.at[pair] for box in boxes[2]))
        inverse = sum(columns(x)[:each] for x in three(1.0 / jnp.where(lanes(total.shape) < each, total, 1.0)))
        partial += dot((acc * inverse).astype(BF16), wo[pair * 128 : (pair + 1) * 128, :])
    mine[...] = partial
    swap = to_partner(2, mine, theirs)
    swap.start()
    swap.wait()
    before = hidden[pl.ds(pl.multiple_of(cell * each, each), each), :].astype(F32) + (mine[...] + theirs[...])
    square = jnp.mean(before * before, axis=-1, keepdims=True)
    normal = (before * lax.rsqrt(square + EPS) * gain[...].reshape(1, D)).astype(BF16)
    for colour in range(COLOURS):
        block = normal[:, colour * 256 : (colour + 1) * 256]
        latents[2 * colour + core, here[0], here[1], here[2]] = jnp.where(core == 0, block[:, :128], block[:, 128:])

    def slab(colour, side, stage, axis=None, digit=None):
        known = GATHER_AXES[colour][stage:]
        at = [here[i] if i in known else slice(None) for i in range(3)]
        if axis is not None:
            at[axis] = digit
        return latents.at[(2 * colour + side,) + tuple(at)]

    def gather_copy(stage, colour, digit):
        axis = GATHER_AXES[colour][stage]
        arrival = last_recv.at[colour, here[axis]] if stage == 2 else gat_recv.at[stage, colour]
        return pltpu.make_async_remote_copy(
            src_ref=slab(colour, core, stage), dst_ref=slab(colour, core, stage),
            send_sem=gat_send.at[stage, colour], recv_sem=arrival,
            device_id=peer(axis, digit), device_id_type=MESH,
        )

    def gather_all(stage, colour):
        part = latents.at[(2 * colour + core,) + (0,) * (2 - stage) + (pl.ds(0, RING - 1),)]
        return pltpu.make_async_remote_copy(
            src_ref=part, dst_ref=part, send_sem=gat_send.at[stage, colour],
            recv_sem=gat_recv.at[min(stage, 1), colour], device_id=partner, device_id_type=MESH,
        )

    def gather_last(colour, digit):
        axis = GATHER_AXES[colour][2]
        return pltpu.make_async_remote_copy(
            src_ref=slab(colour, core, 2), dst_ref=slab(colour, core, 2, axis, digit),
            send_sem=gat_send.at[2, colour], recv_sem=last_recv.at[colour, digit],
            device_id=peer(axis, digit), device_id_type=MESH,
        )

    def forward(colour, part):
        return pltpu.make_async_remote_copy(
            src_ref=part, dst_ref=part, send_sem=fwd_send.at[colour], recv_sem=fwd_recv.at[colour],
            device_id=partner, device_id_type=MESH,
        )

    for stage in range(3):
        for colour in range(COLOURS):
            if stage:
                gather_all(stage - 1, colour).wait_recv()
            axis = GATHER_AXES[colour][stage]
            for step in (2, 1, 3):
                gather_copy(stage, colour, turn(axis, step)).start()
            if stage == 2:
                forward(colour, slab(colour, core, 2)).start()
        for copy in reduce_all(stage):
            copy.wait_send()
    for step in (1, 3, 2):
        for colour in range(COLOURS):
            axis = GATHER_AXES[colour][2]
            digit = turn(axis, step)
            gather_last(colour, digit).wait_recv()
            forward(colour, slab(colour, core, 2, axis, digit)).start()
    for stage in range(2):
        for colour in range(COLOURS):
            gather_all(stage, colour).wait_send()
    for colour in range(COLOURS):
        forward(colour, latents.at[2 * colour + 1 - core]).wait_recv()
    latent = jnp.concatenate([latents[i].reshape(rows, 128) for i in range(2 * COLOURS)], axis=1)
    wide[...] = latent.astype(F32)
    for own, weight in ((k_own, dk), (v_own, dv)):
        projected = dot(latent, weight[...]).astype(BF16)
        for pair in range(COLOURS):
            own[pair] = projected[:, pair * 128 : (pair + 1) * 128]

    def attended(pair, side):
        q = q_own[pair, pl.ds(pl.multiple_of(side * half, half), half)]
        scales = [soft[1, first_head + 2 * pair + part] * HD**-0.5 for part in range(2)]
        return attend(q, k_own[pair], v_own[pair], scales)

    shares = [to_partner(i, att_send.at[pair], att_other.at[pair]) for pair, i in enumerate((1, 3, 4))]
    for pair in range(COLOURS):
        att_send[pair] = attended(pair, 1 - core)
    for copy in shares:
        copy.start()
    for pair in range(COLOURS):
        att[pair] = attended(pair, core)

    for colour in range(COLOURS):
        forward(colour, latents.at[2 * colour + core]).wait_send()
        gather_all(2, colour).wait_send()
    trade.wait()
    for copy in shares:
        copy.wait()


def decoder(wide, att, att_other, o_own, o_other, emb, tally, latent_out, tokens, sem):
    pairs, slots, _ = att.shape
    write = pltpu.make_async_copy(wide, latent_out, sem)
    write.start()
    own = jnp.concatenate([att[i] for i in range(pairs)], axis=1)
    other = jnp.concatenate([att_other[i] for i in range(pairs)], axis=1)
    update = dot(own, o_own[...]) + dot(other, o_other[...])
    position = lax.axis_index("qgrp") * slots + lax.broadcasted_iota(jnp.int32, (slots, 1), 0)
    tokens[...] = jnp.where(position < tally[0], emb[...].astype(F32) + update, 0.0)
    write.wait()


def body(emb, tally, hidden, soft, gq, gk, gv, go, uq, uk, uv, uo, gain):
    rows, group = hidden.shape[0], gq.shape[1]
    slots = emb.shape[0]
    half = slots // 2
    each = rows // RING**3
    dma = pltpu.SemaphoreType.DMA
    held = lambda x: pltpu.VMEM(x.shape, x.dtype)
    emb, hidden, soft, gq, gk, gv, go, uq, uk, uv, uo, gain = (
        pltpu.with_memory_space_constraint(x, pltpu.HBM)
        for x in (emb, hidden, soft, gq, gk, gv, go, uq, uk, uv, uo, gain)
    )
    boxes = []
    for part in (rows // RING, rows // RING**2, each):
        boxes += [
            pltpu.VMEM((COLOURS, RING, part, 128), BF16),
            pltpu.VMEM((COLOURS, RING, 8, max(part, 128)), F32),
        ] * 2
    passed = pl.pallas_call(
        gather,
        name="gather",
        out_shape=(
            jax.ShapeDtypeStruct((rows, D), F32),
            jax.ShapeDtypeStruct((COLOURS, half, 128), BF16),
            jax.ShapeDtypeStruct((COLOURS, half, 128), BF16),
            jax.ShapeDtypeStruct(uo.shape, BF16),
            jax.ShapeDtypeStruct(uo.shape, BF16),
            jax.ShapeDtypeStruct((half, D), BF16),
        ),
        in_specs=[HBM, SMEM] + [HBM] * 11,
        out_specs=(VMEM,) * 6,
        scratch_shapes=[
            pltpu.VMEM((2 * COLOURS, RING, RING, RING, each, 128), BF16),
            held(emb), held(hidden), pltpu.SMEM(soft.shape, F32), held(gq), held(gk), held(gv), held(go), held(gain),
            held(uq), held(uk), held(uv),
            pltpu.VMEM((COLOURS, slots, 128), BF16),
            pltpu.VMEM((COLOURS, rows, 128), BF16),
            pltpu.VMEM((COLOURS, rows, 128), BF16),
            pltpu.VMEM((COLOURS, half, 128), BF16),
            pltpu.VMEM((2 * COLOURS, RING, RING, RING, each, 128), BF16),
            pltpu.VMEM((2 * COLOURS, slots, 128), BF16),
            pltpu.VMEM((COLOURS, slots, 256), BF16),
            *boxes,
            pltpu.VMEM((each, D), F32),
            pltpu.VMEM((each, D), F32),
            dma((12,)), dma((3, 2)), dma((3, 2)), dma((3, COLOURS)), dma((2, COLOURS)), dma((COLOURS, RING)),
            dma((COLOURS,)), dma((COLOURS,)), dma((5,)), dma((5,)),
        ],
        compiler_params=pltpu.CompilerParams(collective_id=0, has_side_effects=True, vmem_limit_bytes=LIMIT),
    )(emb, tally, hidden, soft, gq, gk, gv, go, gain, uq, uk, uv, uo)
    return pl.pallas_call(
        decoder,
        name="decoder",
        out_shape=(jax.ShapeDtypeStruct((rows, D), F32), jax.ShapeDtypeStruct((half, D), F32)),
        in_specs=[VMEM] * 6 + [SMEM],
        out_specs=(HBM, VMEM),
        scratch_shapes=[dma(())],
        compiler_params=pltpu.CompilerParams(vmem_limit_bytes=16 * 1024 * 1024),
    )(*passed, tally)


def solution(mesh):
    column, row = P(None, "qgrp"), P("qgrp", None)
    placed = (P("cell", None), P("cell"), P(), P(), column, column, column, row, column, column, column, row, P())
    return jax.shard_map(
        body,
        mesh=mesh,
        in_specs=placed,
        out_specs=(P(), P(("cell", "qgrp"), None)),
        check_vma=False,
    )
```

```python
import functools
import math

import jax
import jax.numpy as jnp
from jax import lax
from jax.experimental import pallas as pl
from jax.experimental.pallas import tpu as pltpu
from jax.sharding import PartitionSpec as P

D = 768
HEADS = 12
HD = 64
RING = 4
COLOURS = 3
PARTS = 4
REDUCE_AXES = ((0, 1, 2), (1, 2, 0), (2, 0, 1))
GATHER_AXES = ((2, 1, 0), (0, 2, 1), (1, 0, 2))
MASKED = -1e30
EPS = 1e-06
LOG2E = math.log2(math.e)
MESH = pl.DeviceIdType.MESH
F32 = jnp.float32
BF16 = jnp.bfloat16
VMEM = pl.BlockSpec(memory_space=pltpu.VMEM)
SMEM = pl.BlockSpec(memory_space=pltpu.SMEM)
HBM = pl.BlockSpec(memory_space=pltpu.HBM)
LIMIT = 36 * 1024 * 1024


def dot(a, b):
    return jnp.dot(a, b, preferred_element_type=F32)


def dot_nt(a, b):
    return lax.dot_general(a, b, (((1,), (1,)), ((), ())), preferred_element_type=F32)


def lanes(shape):
    return lax.broadcasted_iota(jnp.int32, shape, len(shape) - 1)


def three(x):
    high = x.astype(BF16).astype(F32)
    rest = x - high
    middle = rest.astype(BF16).astype(F32)
    return high, middle, rest - middle


def columns(rows):
    width = rows.shape[1]
    held = jnp.concatenate([rows, jnp.zeros((14, width), F32)], axis=0).astype(BF16)
    head = lax.broadcasted_iota(jnp.int32, (16, 128), 0)
    spread = (lanes((16, 128)) // HD == head).astype(BF16)
    return lax.dot_general(held, spread, (((0,), (0,)), ((), ())), preferred_element_type=F32)


def merged(accs, stats):
    rows = accs.shape[1]
    best = functools.reduce(jnp.maximum, [stats[i, 0:2] for i in range(RING)])
    acc, total = 0.0, 0.0
    for i in range(RING):
        factor = jnp.exp2(stats[i, 0:2] - best).astype(BF16).astype(F32)
        total += factor * stats[i, 2:4]
        acc += columns(factor)[:rows] * accs[i].astype(F32)
    return acc, best, total


def attend(q, k, v, scales):
    first = lanes((1, 128)) < HD
    zero = jnp.zeros_like(k)
    halves = (jnp.where(first, k, zero), jnp.where(first, zero, k))
    widened = jnp.concatenate([v, jnp.ones_like(v)], axis=1)
    tile, results = 128, []
    for start in range(0, q.shape[0], tile):
        mixed = []
        for key, scale in zip(halves, scales):
            scores = dot_nt(q[start : start + tile], key)
            top = jnp.max(scores, axis=-1, keepdims=True)
            weight = jnp.exp2((scores - top) * (scale * LOG2E)).astype(BF16)
            both = dot(weight, widened)
            mixed.append(both[:, :128] / both[:, 128:])
        results.append(jnp.where(first, mixed[0], mixed[1]).astype(BF16))
    return jnp.concatenate(results, axis=0)


def gather(
    emb_h, tally, hidden_h, soft_h, wq_h, wk_h, wv_h, wo_h, gain_h, dq_h, dk_h, dv_h, do_h,
    latents, att, att_other, o_other,
    emb, hidden, soft, wq, wk, wv, wo, gain, dq, dk, dv, q_own, k_own, v_own, att_send,
    q_scr, k_scr, v_scr, *rest,
):
    outs = (rest[0:2], rest[4:6], rest[8:10])
    boxes = (rest[2:4], rest[6:8], rest[10:12])
    mine, theirs, load_sem, red_send, red_recv, gat_send, gat_recv, last_recv, fwd_send, fwd_recv, pair_send, pair_recv = rest[12:]
    cell, core = lax.axis_index("cell"), lax.axis_index("qgrp")
    here = (cell // 16, (cell // 4) % 4, cell % 4)
    partner = (cell, 1 - core)
    rows, group = hidden.shape[0], wq.shape[1]
    slots = emb.shape[0]
    quarter, each = rows // RING, rows // RING**3
    loads = {}
    for i, (name, source, target) in enumerate((
        ("emb", emb_h, emb), ("wk", wk_h, wk), ("wv", wv_h, wv), ("hidden", hidden_h, hidden), ("wq", wq_h, wq),
        ("soft", soft_h, soft), ("dq", dq_h, dq), ("wo", wo_h, wo), ("gain", gain_h, gain),
        ("dk", dk_h, dk), ("dv", dv_h, dv),
    )):
        loads[name] = pltpu.make_async_copy(source, target, load_sem.at[i])
        loads[name].start()

    def ready(*names):
        for name in names:
            loads[name].wait()

    def peer(axis, digit):
        at = [digit if i == axis else here[i] for i in range(3)]
        return ((at[0] * RING + at[1]) * RING + at[2], core)

    def turn(axis, step):
        return lax.rem(here[axis] + step, RING)

    def to_partner(i, source, target):
        return pltpu.make_async_remote_copy(
            src_ref=source, dst_ref=target, send_sem=pair_send.at[i], recv_sem=pair_recv.at[i],
            device_id=partner, device_id_type=MESH,
        )

    barrier = pltpu.get_barrier_semaphore()
    for axis in range(3):
        for step in range(1, RING):
            pl.semaphore_signal(barrier, inc=1, device_id=peer(axis, turn(axis, step)), device_id_type=MESH)
    pl.semaphore_signal(barrier, inc=1, device_id=partner, device_id_type=MESH)

    first_head = core * (2 * COLOURS)
    first = lanes((1, 128)) < HD
    valid = lax.broadcasted_iota(jnp.int32, (slots, 1), 0) < tally[0]
    ready("emb", "wk", "soft", "wv")
    keys = dot(emb[...], wk[...]).astype(BF16).astype(F32)
    keys = jnp.where(valid, keys, keys[0:1])
    for pair in range(COLOURS):
        scale = [soft[0, first_head + 2 * pair + part] * (HD**-0.5 * LOG2E) for part in range(2)]
        scaled = keys[:, pair * 128 : (pair + 1) * 128] * jnp.where(first, scale[0], scale[1])
        high = scaled.astype(BF16).astype(F32)
        rest = scaled - high
        k_scr[2 * pair] = jnp.where(first, high, pltpu.roll(rest, HD, 1)).astype(BF16)
        k_scr[2 * pair + 1] = jnp.where(first, pltpu.roll(high, HD, 1), rest).astype(BF16)
    values = jnp.where(valid, dot(emb[...], wv[...]), 0.0).astype(BF16)
    for pair in range(COLOURS):
        v_scr[pair, :, :128] = values[:, pair * 128 : (pair + 1) * 128]
        v_scr[pair, :, 128:] = jnp.broadcast_to(jnp.where(valid, 1.0, 0.0), (slots, 128)).astype(BF16)
    ready("hidden", "wq")
    queries = dot(hidden[...], wq[...])
    for pair in range(COLOURS):
        one = queries[:, pair * 128 : (pair + 1) * 128]
        other = pltpu.roll(one, HD, 1)
        for part in range(2):
            double = jnp.where(first == (part == 0), one, other).astype(BF16)
            q_scr[2 * pair + part] = double.reshape(RING, RING, RING, each, 128)

    pl.semaphore_wait(barrier, 10)
    trade = to_partner(0, do_h, o_other)
    trade.start()

    def tile(pair, digit):
        axis, following, _ = REDUCE_AXES[pair]
        rest = [i for i in range(3) if i != axis]
        where = tuple(digit if i == axis else slice(None) for i in range(axis + 1))
        tops, both = [], []
        for part in range(2):
            q = q_scr[(2 * pair + part,) + where]
            if rest[0] != following:
                q = jnp.concatenate([q[:, i].reshape(RING * each, 128) for i in range(RING)], axis=0)
            scores = dot_nt(q.reshape(quarter, 128), k_scr[2 * pair + part])
            tops.append(jnp.max(scores, axis=-1, keepdims=True))
            both.append(dot(jnp.exp2(scores - tops[-1]).astype(BF16), v_scr[pair]))
        acc = jnp.where(first, both[0][:, :128], both[1][:, :128]).astype(BF16)
        lane = lanes((1, 128))
        stats = jnp.where(lane == 0, tops[0], jnp.where(lane == 1, tops[1], jnp.where(lane == 2, both[0][:, 128:], both[1][:, 128:])))
        return acc, stats.T[0:8]

    def reduce_copy(stage, pair, digit):
        axis = REDUCE_AXES[pair][stage]
        return [
            pltpu.make_async_remote_copy(
                src_ref=outs[stage][i].at[pair, digit], dst_ref=boxes[stage][i].at[pair, here[axis]],
                send_sem=red_send.at[stage, i], recv_sem=red_recv.at[stage, i],
                device_id=peer(axis, digit), device_id_type=MESH,
            )
            for i in range(2)
        ]

    def reduce_all(stage):
        return [
            pltpu.make_async_remote_copy(
                src_ref=outs[stage][i].at[:, pl.ds(0, RING - 1)], dst_ref=boxes[stage][i].at[:, pl.ds(0, RING - 1)],
                send_sem=red_send.at[stage, i], recv_sem=red_recv.at[stage, i],
                device_id=partner, device_id_type=MESH,
            )
            for i in range(2)
        ]

    @pl.loop(0, RING - 1)
    def _(i):
        step = lax.rem(2 + i + i * (i - 1) // 2, RING)
        digits = [turn(REDUCE_AXES[pair][0], step) for pair in range(COLOURS)]
        for pair in range(COLOURS):
            outs[0][0][pair, digits[pair]], outs[0][1][pair, digits[pair]] = tile(pair, digits[pair])
        for pair in range(COLOURS):
            for copy in reduce_copy(0, pair, digits[pair]):
                copy.start()

    for pair in range(COLOURS):
        own = here[REDUCE_AXES[pair][0]]
        boxes[0][0][pair, own], boxes[0][1][pair, own] = tile(pair, own)

    half = slots // 2
    ready("dq", "wo", "gain", "dk", "dv")
    projected = dot(emb[...], dq[...]).astype(BF16)
    for pair in range(COLOURS):
        q_own[pair] = projected[:, pair * 128 : (pair + 1) * 128]

    for stage in (1, 2):
        for copy in reduce_all(stage - 1):
            copy.wait_recv()
        part = rows // RING ** (stage + 1)
        for pair in range(COLOURS):
            acc, top, total = merged(*(box.at[pair] for box in boxes[stage - 1]))
            stats = jnp.concatenate([top, total, jnp.zeros((4, top.shape[1]), F32)], axis=0)
            for i in range(RING):
                outs[stage][0][pair, i] = acc[i * part : (i + 1) * part].astype(BF16)
                outs[stage][1][pair, i] = jnp.concatenate(
                    [stats[:, i * part : (i + 1) * part], jnp.zeros((8, 128 - part), F32)], axis=1
                )
        for pair in range(COLOURS):
            axis = REDUCE_AXES[pair][stage]
            for step in (2, 1, 3):
                for copy in reduce_copy(stage, pair, turn(axis, step)):
                    copy.start()
        for pair in range(COLOURS):
            own = here[REDUCE_AXES[pair][stage]]
            for i in range(2):
                boxes[stage][i][pair, own] = outs[stage][i][pair, own]

    for copy in reduce_all(2):
        copy.wait_recv()
    partial = jnp.zeros((each, D), F32)
    for pair in range(COLOURS):
        acc, _, total = merged(*(box.at[pair] for box in boxes[2]))
        inverse = sum(columns(x)[:each] for x in three(1.0 / jnp.where(lanes(total.shape) < each, total, 1.0)))
        partial += dot((acc * inverse).astype(BF16), wo[pair * 128 : (pair + 1) * 128, :])
    mine[...] = partial
    swap = to_partner(2, mine, theirs)
    swap.start()
    swap.wait()
    before = hidden[pl.ds(pl.multiple_of(cell * each, each), each), :].astype(F32) + (mine[...] + theirs[...])
    square = jnp.mean(before * before, axis=-1, keepdims=True)
    normal = (before * lax.rsqrt(square + EPS) * gain[...].reshape(1, D)).astype(BF16)
    for colour in range(COLOURS):
        block = normal[:, colour * 256 : (colour + 1) * 256]
        latents[2 * colour + core, here[0], here[1], here[2]] = jnp.where(core == 0, block[:, :128], block[:, 128:])

    def slab(colour, side, stage, axis=None, digit=None):
        known = GATHER_AXES[colour][stage:]
        at = [here[i] if i in known else slice(None) for i in range(3)]
        if axis is not None:
            at[axis] = digit
        return latents.at[(2 * colour + side,) + tuple(at)]

    def gather_copy(stage, colour, digit):
        axis = GATHER_AXES[colour][stage]
        arrival = last_recv.at[colour, here[axis]] if stage == 2 else gat_recv.at[stage, colour]
        return pltpu.make_async_remote_copy(
            src_ref=slab(colour, core, stage), dst_ref=slab(colour, core, stage),
            send_sem=gat_send.at[stage, colour], recv_sem=arrival,
            device_id=peer(axis, digit), device_id_type=MESH,
        )

    def gather_all(stage, colour):
        part = latents.at[(2 * colour + core,) + (0,) * (2 - stage) + (pl.ds(0, RING - 1),)]
        return pltpu.make_async_remote_copy(
            src_ref=part, dst_ref=part, send_sem=gat_send.at[stage, colour],
            recv_sem=gat_recv.at[min(stage, 1), colour], device_id=partner, device_id_type=MESH,
        )

    def gather_last(colour, digit):
        axis = GATHER_AXES[colour][2]
        return pltpu.make_async_remote_copy(
            src_ref=slab(colour, core, 2), dst_ref=slab(colour, core, 2, axis, digit),
            send_sem=gat_send.at[2, colour], recv_sem=last_recv.at[colour, digit],
            device_id=peer(axis, digit), device_id_type=MESH,
        )

    def forward(colour, part):
        return pltpu.make_async_remote_copy(
            src_ref=part, dst_ref=part, send_sem=fwd_send.at[colour], recv_sem=fwd_recv.at[colour],
            device_id=partner, device_id_type=MESH,
        )

    for stage in range(3):
        for colour in range(COLOURS):
            if stage:
                gather_all(stage - 1, colour).wait_recv()
            axis = GATHER_AXES[colour][stage]
            for step in (2, 1, 3):
                gather_copy(stage, colour, turn(axis, step)).start()
            if stage == 2:
                forward(colour, slab(colour, core, 2)).start()
        for copy in reduce_all(stage):
            copy.wait_send()
    for step in (1, 3, 2):
        for colour in range(COLOURS):
            axis = GATHER_AXES[colour][2]
            digit = turn(axis, step)
            gather_last(colour, digit).wait_recv()
            forward(colour, slab(colour, core, 2, axis, digit)).start()
    for stage in range(2):
        for colour in range(COLOURS):
            gather_all(stage, colour).wait_send()
    for colour in range(COLOURS):
        forward(colour, latents.at[2 * colour + 1 - core]).wait_recv()
    latent = jnp.concatenate([latents[i].reshape(rows, 128) for i in range(2 * COLOURS)], axis=1)
    for own, weight in ((k_own, dk), (v_own, dv)):
        projected = dot(latent, weight[...]).astype(BF16)
        for pair in range(COLOURS):
            own[pair] = projected[:, pair * 128 : (pair + 1) * 128]

    def attended(pair, side):
        q = q_own[pair, pl.ds(pl.multiple_of(side * half, half), half)]
        scales = [soft[1, first_head + 2 * pair + part] * HD**-0.5 for part in range(2)]
        return attend(q, k_own[pair], v_own[pair], scales)

    shares = [to_partner(i, att_send.at[pair], att_other.at[pair]) for pair, i in enumerate((1, 3, 4))]
    for pair in range(COLOURS):
        att_send[pair] = attended(pair, 1 - core)
    for copy in shares:
        copy.start()
    for pair in range(COLOURS):
        att[pair] = attended(pair, core)

    for colour in range(COLOURS):
        forward(colour, latents.at[2 * colour + core]).wait_send()
        gather_all(2, colour).wait_send()
    trade.wait()
    for copy in shares:
        copy.wait()


def decoder(
    lat, att, att_other, o_other, emb_h, tally, o_own_h,
    latent_out, tokens, emb, o_own, wide, sem,
):
    core = lax.axis_index("qgrp")
    blocks = lat.shape[0]
    pairs, slots, _ = att.shape
    loads = [
        pltpu.make_async_copy(emb_h.at[pl.ds(pl.multiple_of(core * slots, slots), slots)], emb, sem.at[0]),
        pltpu.make_async_copy(o_own_h, o_own, sem.at[1]),
    ]
    for copy in loads:
        copy.start()
    part = wide.shape[0] // PARTS
    writes = []
    for r in range(PARTS):
        for i in range(blocks):
            wide[r * part : (r + 1) * part, i * 128 : (i + 1) * 128] = lat[i, r * part : (r + 1) * part].astype(F32)
        at = pl.ds(r * part, part)
        writes.append(pltpu.make_async_copy(wide.at[at], latent_out.at[at], sem.at[2 + r]))
        writes[-1].start()
    for copy in loads:
        copy.wait()
    own = jnp.concatenate([att[i] for i in range(pairs)], axis=1)
    other = jnp.concatenate([att_other[i] for i in range(pairs)], axis=1)
    update = dot(own, o_own[...]) + dot(other, o_other[...])
    position = core * slots + lax.broadcasted_iota(jnp.int32, (slots, 1), 0)
    tokens[...] = jnp.where(position < tally[0], emb[...].astype(F32) + update, 0.0)
    for copy in writes:
        copy.wait()


def body(emb, tally, hidden, soft, gq, gk, gv, go, uq, uk, uv, uo, gain):
    rows, group = hidden.shape[0], gq.shape[1]
    slots = emb.shape[0]
    half = slots // 2
    each = rows // RING**3
    dma = pltpu.SemaphoreType.DMA
    held = lambda x: pltpu.VMEM(x.shape, x.dtype)
    emb, hidden, soft, gq, gk, gv, go, uq, uk, uv, uo, gain = (
        pltpu.with_memory_space_constraint(x, pltpu.HBM)
        for x in (emb, hidden, soft, gq, gk, gv, go, uq, uk, uv, uo, gain)
    )
    boxes = []
    for part in (rows // RING, rows // RING**2, each):
        boxes += [
            pltpu.VMEM((COLOURS, RING, part, 128), BF16),
            pltpu.VMEM((COLOURS, RING, 8, max(part, 128)), F32),
        ] * 2
    latents, att, att_other, o_other = pl.pallas_call(
        gather,
        name="gather",
        out_shape=(
            jax.ShapeDtypeStruct((2 * COLOURS, RING, RING, RING, each, 128), BF16),
            jax.ShapeDtypeStruct((COLOURS, half, 128), BF16),
            jax.ShapeDtypeStruct((COLOURS, half, 128), BF16),
            jax.ShapeDtypeStruct(uo.shape, BF16),
        ),
        in_specs=[HBM, SMEM] + [HBM] * 11,
        out_specs=(VMEM,) * 4,
        scratch_shapes=[
            held(emb), held(hidden), pltpu.SMEM(soft.shape, F32), held(gq), held(gk), held(gv), held(go), held(gain),
            held(uq), held(uk), held(uv),
            pltpu.VMEM((COLOURS, slots, 128), BF16),
            pltpu.VMEM((COLOURS, rows, 128), BF16),
            pltpu.VMEM((COLOURS, rows, 128), BF16),
            pltpu.VMEM((COLOURS, half, 128), BF16),
            pltpu.VMEM((2 * COLOURS, RING, RING, RING, each, 128), BF16),
            pltpu.VMEM((2 * COLOURS, slots, 128), BF16),
            pltpu.VMEM((COLOURS, slots, 256), BF16),
            *boxes,
            pltpu.VMEM((each, D), F32),
            pltpu.VMEM((each, D), F32),
            dma((11,)), dma((3, 2)), dma((3, 2)), dma((3, COLOURS)), dma((2, COLOURS)), dma((COLOURS, RING)),
            dma((COLOURS,)), dma((COLOURS,)), dma((5,)), dma((5,)),
        ],
        compiler_params=pltpu.CompilerParams(collective_id=0, has_side_effects=True, vmem_limit_bytes=LIMIT),
    )(emb, tally, hidden, soft, gq, gk, gv, go, gain, uq, uk, uv, uo)
    return pl.pallas_call(
        decoder,
        name="decoder",
        out_shape=(jax.ShapeDtypeStruct((rows, D), F32), jax.ShapeDtypeStruct((half, D), F32)),
        in_specs=[VMEM] * 4 + [HBM, SMEM, HBM],
        out_specs=(HBM, VMEM),
        scratch_shapes=[pltpu.VMEM((half, D), BF16), held(uo), pltpu.VMEM((rows, D), F32), dma((2 + PARTS,))],
        compiler_params=pltpu.CompilerParams(vmem_limit_bytes=LIMIT),
    )(latents.reshape(2 * COLOURS, rows, 128), att, att_other, o_other, emb, tally, uo)


def solution(mesh):
    column, row = P(None, "qgrp"), P("qgrp", None)
    placed = (P("cell", None), P("cell"), P(), P(), column, column, column, row, column, column, column, row, P())
    return jax.shard_map(
        body,
        mesh=mesh,
        in_specs=placed,
        out_specs=(P(), P(("cell", "qgrp"), None)),
        check_vma=False,
    )
```
